32 devices in a mesh: cfg: 2 (over y), tm: 16 (over z, x, core).
Axes of the slice: x: 2, y: 2, z: 4, core: 2. Of those that a mesh axis runs over, the one named last changes fastest.
Arguments:
- meson_fields: bfloat16 [2, 32, 32, 256, 256], P(None, None, ('cfg', 'tm')), parts along dimension 2, may hold values from -1.3 to 1.3
- perambulators: bfloat16 [2, 32, 256, 256], P(None, ('cfg', 'tm')), parts along dimension 1, may hold values from -0.25 to 0.25
- direct_ins: int32 [4096, 4], replicated, may hold values from 0 to 31, as said below
- direct_coef: float32 [4096], replicated, may hold values from -5 to 5
- direct_entry: int32 [4096], replicated, may hold values from 0 to 63
- box_ins: int32 [8, 4], replicated, may hold values from 0 to 31, as said below
- box_coef: float32 [8], replicated, may hold values from -24 to 24
- box_entry: int32 [8], replicated, may hold values from 0 to 63
Outputs:
- correlator: float32 [3, 2, 128], P(None, None, ('cfg', 'tm')), parts along dimension 2
The draws below stay inside these ranges and needn't reach their ends.
There are 2 independent parts, one for each index of `cfg`. The reference program is written for one: setup_inputs(seed, part) draws one part's arguments, and reference() takes and returns one part's arrays. A program takes and returns all parts, laid end to end along the dimension named above; an argument that names none is the same for every part. Nothing has to cross between parts.
Inputs may be any that keep to these rules, and one draw needn't show every extreme that they name: `direct_ins`: within a term, insertions 0 and 1 differ, 1 and 2 differ, 2 and 3 differ. `box_ins`: within a term, insertions 0 and 1 differ, 1 and 2 differ, 2 and 3 differ.
All inputs are finite; a program needn't handle non-finite values.
Results may differ from the reference program's by a relative error of at most 0.0046.
Values may be sent and summed in bfloat16 or wider, within the bound.
No kernel may reach another device: no remote copies, remote signals or barrier semaphores. Data moves between devices by JAX's collectives and lax.ppermute only.
A program may use at most 192 MiB of HBM per device.

```python
import math
import jax
import jax.numpy as jnp
from jax import lax

MODES = 256
INSERTIONS = 32
SLICE_DEV = 1
SLICES = 16
SEPARATIONS = 3
DIRECT_TERMS = 4096
BOX_TERMS = 8
ENTRIES = 64


def draw_meson_fields(key, part):
    subkeys = jax.random.split(key, 3)
    field_shape = (2, INSERTIONS, SLICES, MODES, MODES)
    spread = math.sqrt(10.0)
    base_draw = jax.random.truncated_normal(subkeys[0], -6.0, 6.0, field_shape, jnp.float32)
    row_scale = jnp.exp(jax.random.uniform(subkeys[1], (1, INSERTIONS, SLICES, MODES, 1), jnp.float32, 0.0, math.log(spread)))
    col_scale = jnp.exp(jax.random.uniform(subkeys[2], (1, INSERTIONS, SLICES, 1, MODES), jnp.float32, 0.0, math.log(spread)))
    mean_square = (spread * spread - 1.0) / (2.0 * math.log(spread))
    time_ramp = jnp.arange(SLICES, dtype=jnp.float32) / max(SLICES - 1, 1)
    time_scale = jnp.exp(0.25 * math.log(3.0) * time_ramp)[None, None, :, None, None]
    values = base_draw * row_scale * col_scale * time_scale / (mean_square * math.sqrt(MODES))
    return jnp.clip(values, -1.3, 1.3).astype(jnp.bfloat16)


def draw_terms(key, term_count):
    subkeys = jax.random.split(key, 3)
    leading = jax.random.randint(subkeys[0], (term_count,), 0, INSERTIONS)
    placed = jax.random.permutation(subkeys[1], term_count)
    position = jnp.arange(term_count)
    leading = jnp.where(position == placed[0], 0, jnp.where(position == placed[1], INSERTIONS - 1, leading))
    offsets = jax.random.randint(subkeys[2], (term_count, 3), 1, INSERTIONS)
    second = (leading + offsets[:, 0]) % INSERTIONS
    third_ins = (second + offsets[:, 1]) % INSERTIONS
    fourth = (third_ins + offsets[:, 2]) % INSERTIONS
    return jnp.stack([leading, second, third_ins, fourth], axis=1).astype(jnp.int32)


def draw_direct_ins(key, part):
    return draw_terms(jax.random.fold_in(key, 17), DIRECT_TERMS)


def draw_box_ins(key, part):
    return draw_terms(jax.random.fold_in(key, 29), BOX_TERMS)


def place_ends(entries, rng, low, largest):
    longest = entries.shape.index(max(entries.shape))
    spots = []
    for shift in (0, 1):
        where = [jax.random.randint(jax.random.fold_in(rng, axis), (), 0, length) for axis, length in enumerate(entries.shape)]
        where[longest] = (where[longest] + shift) % entries.shape[longest]
        spots.append(tuple(where))
    return entries.at[spots[0]].set(low).at[spots[1]].set(largest)


def level_of(own_key, shape, cuts, smallest, largest):
    factor_of, own = 1.0, jax.random.fold_in(own_key, 6)
    for dim, parts in cuts:
        steps = jnp.exp(jax.random.uniform(jax.random.fold_in(own, dim), (parts,), jnp.float32, smallest / len(cuts), largest / len(cuts)))
        factor_of = factor_of * jnp.repeat(steps, shape[dim] // parts).reshape([-1 if axis == dim else 1 for axis in range(len(shape))])
    return factor_of


def normal_values(stream_key, dims, width, reach, shards=(), kind=jnp.bfloat16):
    gain = level_of(stream_key, dims, shards, -0.22, 0.18) if shards else 1.0
    entries = jax.random.normal(stream_key, dims, jnp.float32) * width * gain
    return jnp.minimum(jnp.maximum(entries, -reach), reach).astype(kind)


def setup_inputs(seed: int = 0, part: int = 0) -> dict:
    streams_of = jax.random.split(jax.random.key(seed), 9)
    own_keys = jax.random.split(jax.random.fold_in(streams_of[8], part), 9)
    return {
        "meson_fields": draw_meson_fields(jax.random.fold_in(jax.random.fold_in(streams_of[8], part), 71), part),
        "perambulators": normal_values(own_keys[1], (2, SLICES, MODES, MODES), (2 * MODES) ** -0.5, 0.25, ((1, 16),)),
        "direct_ins": draw_direct_ins(jax.random.fold_in(streams_of[8], 71), part),
        "direct_coef": normal_values(streams_of[3], (DIRECT_TERMS,), 1.0, 5.0, (), jnp.float32),
        "direct_entry": place_ends(jax.random.randint(streams_of[4], (DIRECT_TERMS,), 0, ENTRIES), jax.random.fold_in(streams_of[4], 1), 0, ENTRIES - 1).astype(jnp.int32),
        "box_ins": draw_box_ins(jax.random.fold_in(streams_of[8], 71), part),
        "box_coef": normal_values(streams_of[6], (BOX_TERMS,), 4.0, 24.0, (), jnp.float32),
        "box_entry": place_ends(jax.random.randint(streams_of[7], (BOX_TERMS,), 0, ENTRIES), jax.random.fold_in(streams_of[7], 1), 0, ENTRIES - 1).astype(jnp.int32),
    }


def dress(fields, propagator):
    stacked = jnp.stack([jnp.stack([propagator[0], propagator[1]], 1), jnp.stack([-propagator[1], propagator[0]], 1)], 0)
    product = jnp.einsum("cgij,cjdk->dgik", fields.astype(jnp.float32), stacked.astype(jnp.float32))
    return product.astype(jnp.bfloat16)


def adjoint_product(left_side, right_side):
    real_part = jnp.einsum("clij,clkj->lik", left_side, right_side)
    imag_part = jnp.einsum("lij,lkj->lik", left_side[1], right_side[0]) - jnp.einsum("lij,lkj->lik", left_side[0], right_side[1])
    return real_part, imag_part


def pair_terms(sink_side, source, direct_ins, direct_coef, direct_entry, box_ins, box_coef, box_entry):
    sink_side = sink_side.astype(jnp.float32)
    source = source.astype(jnp.float32)
    loop_real = jnp.einsum("cgij,chij->gh", sink_side, source)
    loop_imag = jnp.einsum("gij,hij->gh", sink_side[1], source[0]) - jnp.einsum("gij,hij->gh", sink_side[0], source[1])
    real_left = loop_real[direct_ins[:, 0], direct_ins[:, 1]]
    imag_left = loop_imag[direct_ins[:, 0], direct_ins[:, 1]]
    real_right = loop_real[direct_ins[:, 2], direct_ins[:, 3]]
    imag_right = loop_imag[direct_ins[:, 2], direct_ins[:, 3]]
    direct_real = direct_coef * (real_left * real_right - imag_left * imag_right)
    direct_imag = direct_coef * (real_left * imag_right + imag_left * real_right)
    first_real, first_imag = adjoint_product(sink_side[:, box_ins[:, 0]], source[:, box_ins[:, 1]])
    second_real, second_imag = adjoint_product(source[:, box_ins[:, 3]], sink_side[:, box_ins[:, 2]])
    box_real = box_coef * jnp.sum(first_real * second_real + first_imag * second_imag, axis=(1, 2))
    box_imag = box_coef * jnp.sum(first_imag * second_real - first_real * second_imag, axis=(1, 2))
    direct_sum = jax.ops.segment_sum(jnp.stack([direct_real, direct_imag], 1), direct_entry, num_segments=ENTRIES)
    box_sum = jax.ops.segment_sum(jnp.stack([box_real, box_imag], 1), box_entry, num_segments=ENTRIES)
    return jnp.transpose(direct_sum - box_sum)


def reference(meson_fields, perambulators, direct_ins, direct_coef, direct_entry, box_ins, box_coef, box_entry):
    dressed = lax.map(lambda pieces: dress(pieces[0], pieces[1]), (jnp.moveaxis(meson_fields, 2, 0), jnp.moveaxis(perambulators, 1, 0)))
    outputs = []
    for distance in range(SEPARATIONS):
        def accumulate(totals, sink_time):
            source_time = ((sink_time + distance * SLICE_DEV) % SLICES).astype(jnp.int32)
            added = pair_terms(dressed[sink_time], dressed[source_time], direct_ins, direct_coef, direct_entry, box_ins, box_coef, box_entry)
            return totals + added, None
        totals, unused = lax.scan(accumulate, jnp.zeros((2, ENTRIES), jnp.float32), jnp.arange(SLICES, dtype=jnp.int32))
        outputs.append(totals / SLICES)
    return jnp.stack(outputs)
```

```python
import functools

import jax
import jax.numpy as jnp
from jax import lax
from jax.experimental import pallas as pl
from jax.experimental.pallas import tpu as pltpu
from jax.sharding import PartitionSpec as P

CHUNKS = 4
GROUP = 4
STEP_ROWS = 16
STEP_INS = 8
LANES = 128
TERM_STEP = 512
NT = (((1,), (1,)), ((), ()))


def nt_dot(left, right):
    return lax.dot_general(left, right, NT, preferred_element_type=jnp.float32)


def dress_kernel(fields, factor, out, weight):
    modes = factor.shape[-1]

    @pl.when(pl.program_id(0) == 0)
    def _():
        weight[:modes, :modes] = factor[0]
        weight[:modes, modes:] = factor[1]
        weight[modes:, :modes] = -factor[1]
        weight[modes:, modes:] = factor[0]

    inserts, rows = fields.shape[1:3]
    real_side = fields[0].reshape(inserts * rows, modes)
    imag_side = fields[1].reshape(inserts * rows, modes)
    product = jnp.dot(real_side, weight[:modes], preferred_element_type=jnp.float32)
    product += jnp.dot(imag_side, weight[modes:], preferred_element_type=jnp.float32)
    product = product.astype(out.dtype)
    out[0] = product[:, :modes].reshape(inserts, rows, modes)
    out[1] = product[:, modes:].reshape(inserts, rows, modes)


def dress(fields, factor, chunk):
    inserts, modes = fields.shape[1], fields.shape[-1]
    rows = modes // CHUNKS
    return pl.pallas_call(
        dress_kernel,
        grid=(inserts // STEP_INS,),
        in_specs=[
            pl.BlockSpec((2, STEP_INS, rows, modes), lambda g: (0, g, chunk, 0)),
            pl.BlockSpec((2, modes, modes), lambda g: (0, 0, 0)),
        ],
        out_specs=pl.BlockSpec((2, STEP_INS, rows, modes), lambda g: (0, g, 0, 0)),
        out_shape=jax.ShapeDtypeStruct((2, inserts, rows, modes), fields.dtype),
        scratch_shapes=[pltpu.VMEM((2 * modes, 2 * modes), fields.dtype)],
        cost_estimate=pl.CostEstimate(
            flops=16 * inserts * rows * modes * modes,
            bytes_accessed=8 * inserts * rows * modes,
            transcendentals=0,
        ),
        name="dress",
    )(fields, factor)


def gram_kernel(count, left_count, *refs):
    blocks, out, turned, flat = refs[:count], refs[count], refs[count + 1], refs[count + 2]
    _, inserts, rows, modes = blocks[0].shape
    size = 2 * inserts
    halves = modes // LANES
    for index, block in enumerate(blocks):
        for place in range(size):
            piece = block[place // inserts, place % inserts].astype(jnp.float32)
            for half in range(halves):
                turned[half, pl.ds(place, rows, stride=size), :] = piece[
                    :, half * LANES : (half + 1) * LANES
                ]
        for row in range(rows):
            for half in range(halves):
                column = row * modes + half * LANES
                flat[index * size : (index + 1) * size, column : column + LANES] = turned[
                    half, row * size : (row + 1) * size, :
                ].astype(flat.dtype)
    product = nt_dot(flat[: left_count * size], flat[...])

    @pl.when(pl.program_id(0) == 0)
    def _():
        out[...] = product

    @pl.when(pl.program_id(0) > 0)
    def _():
        out[...] += product


def gram(blocks, left_count):
    count = len(blocks)
    _, inserts, rows, modes = blocks[0].shape
    size = 2 * inserts
    spec = pl.BlockSpec((2, inserts, STEP_ROWS, modes), lambda i: (0, 0, i, 0))
    shape = (left_count * size, count * size)
    return pl.pallas_call(
        functools.partial(gram_kernel, count, left_count),
        grid=(rows // STEP_ROWS,),
        in_specs=[spec] * count,
        out_specs=pl.BlockSpec(shape, lambda i: (0, 0)),
        out_shape=jax.ShapeDtypeStruct(shape, jnp.float32),
        scratch_shapes=[
            pltpu.VMEM((modes // LANES, STEP_ROWS * size, LANES), jnp.float32),
            pltpu.VMEM((count * size, STEP_ROWS * modes), jnp.bfloat16),
        ],
        cost_estimate=pl.CostEstimate(
            flops=16 * shape[0] * shape[1] * rows * modes,
            bytes_accessed=count * 2 * size * rows * modes,
            transcendentals=0,
        ),
        name="gram",
    )(*blocks)


def box_kernel(pieces, ins, entry, coef, weight, *refs):
    out = refs[-1]
    groups = [refs[place * pieces : (place + 1) * pieces] for place in range(4)]

    def whole(group, part):
        return jnp.concatenate([ref[part, 0] for ref in group], axis=0)

    def both(group):
        return whole(group, 0), whole(group, 1)

    def product(left, right):
        left_real, left_imag = both(left)
        right_real, right_imag = both(right)
        right_side = jnp.concatenate([right_real, right_imag], axis=1)
        real = nt_dot(jnp.concatenate([left_real, left_imag], axis=1), right_side)
        imag = nt_dot(jnp.concatenate([left_imag, -left_real], axis=1), right_side)
        return real, imag

    term = pl.program_id(0)
    first_real, first_imag = product(groups[0], groups[1])
    second_real, second_imag = product(groups[3], groups[2])
    real = jnp.sum(first_real * second_real + first_imag * second_imag) * coef[term]
    imag = jnp.sum(first_imag * second_real - first_real * second_imag) * coef[term]
    imag = imag * weight[3]
    here = lax.broadcasted_iota(jnp.int32, out.shape, 1) == entry[term]
    line = lax.broadcasted_iota(jnp.int32, out.shape, 0)
    added = jnp.zeros(out.shape, jnp.float32)
    for apart in range(3):
        added = jnp.where(line == 2 * apart, real * weight[apart], added)
        added = jnp.where(line == 2 * apart + 1, imag * weight[apart], added)
    added = jnp.where(here, added, 0.0)

    @pl.when(term == 0)
    def _():
        out[...] = added

    @pl.when(term > 0)
    def _():
        out[...] += added


def box(left, right, ins, entry, coef, weight, entries, slots=0):
    pieces = len(left)
    terms = ins.shape[1]
    rows, modes = left[0].shape[2:]
    operands, specs = [], []
    for place in range(4):
        for number, piece in enumerate(left if place % 2 == 0 else right):
            if place % 2 == 0 and number >= pieces - slots:
                offset = (place // 2) * terms
                specs.append(
                    pl.BlockSpec(
                        (2, 1, rows, modes),
                        lambda l, ins, entry, coef, weight, offset=offset: (0, offset + l, 0, 0),
                    )
                )
            else:
                specs.append(
                    pl.BlockSpec(
                        (2, 1, rows, modes),
                        lambda l, ins, entry, coef, weight, place=place: (0, ins[place, l], 0, 0),
                    )
                )
            operands.append(piece)
    return pl.pallas_call(
        functools.partial(box_kernel, pieces),
        grid_spec=pltpu.PrefetchScalarGridSpec(
            num_scalar_prefetch=4,
            grid=(terms,),
            in_specs=specs,
            out_specs=pl.BlockSpec((8, entries), lambda l, *refs: (0, 0)),
        ),
        out_shape=jax.ShapeDtypeStruct((8, entries), jnp.float32),
        cost_estimate=pl.CostEstimate(
            flops=16 * terms * modes * modes * modes,
            bytes_accessed=16 * terms * modes * modes,
            transcendentals=0,
        ),
        name="box",
    )(ins, entry, coef, weight, *operands)


def pick_kernel(upper, ins, *refs):
    del ins
    blocks, out = refs[:-1], refs[-1]
    half = len(blocks) // 2

    @pl.when(upper[0] == 1)
    def _():
        for number in range(half):
            out[number] = blocks[half + number][...]

    @pl.when(upper[0] == 0)
    def _():
        for number in range(half):
            out[number] = blocks[number][...]


def pick(blocks, places, upper):
    _, _, rows, modes = blocks[0].shape
    half, count = len(blocks) // 2, places.shape[0]
    spec = pl.BlockSpec((2, 1, rows, modes), lambda l, upper, ins: (0, ins[l], 0, 0))
    return pl.pallas_call(
        pick_kernel,
        grid_spec=pltpu.PrefetchScalarGridSpec(
            num_scalar_prefetch=2,
            grid=(count,),
            in_specs=[spec] * len(blocks),
            out_specs=pl.BlockSpec(
                (half, 2, 1, rows, modes), lambda l, upper, ins: (0, 0, l, 0, 0)
            ),
        ),
        out_shape=jax.ShapeDtypeStruct((half, 2, count, rows, modes), blocks[0].dtype),
        name="pick",
    )(upper, places, *blocks)


def thirds(value, axis):
    high = value.astype(jnp.bfloat16)
    rest = value - high.astype(jnp.float32)
    middle = rest.astype(jnp.bfloat16)
    low = (rest - middle.astype(jnp.float32)).astype(jnp.bfloat16)
    return jnp.concatenate([high, middle, low], axis=axis)


def direct_kernel(swap, weight, ins, coef, entry, *refs):
    grams, out, lines = refs[:-2], refs[-2], refs[-1]
    pairs = len(grams)
    size = grams[0].shape[0]
    inserts = size // 2
    for pair, ref in enumerate(grams):
        table = ref[...]
        table = jnp.where(swap[pair] == 1, table.T, table)
        upper, lower = table[:inserts], table[inserts:]
        real = upper[:, :inserts] + lower[:, inserts:]
        imag = lower[:, :inserts] - upper[:, inserts:]
        lines[pair * size : pair * size + inserts] = real
        lines[pair * size + inserts : (pair + 1) * size] = imag
    table = thirds(lines[...], 1)
    entries = out.shape[1]
    total = jnp.zeros(out.shape, jnp.float32)
    step = min(TERM_STEP, ins.shape[1])
    for start in range(0, ins.shape[1], step):
        span = slice(start, start + step)
        places = lax.broadcasted_iota(jnp.int32, (inserts, step), 0)

        def values(left, right):
            chosen = (places == ins[right : right + 1, span]).astype(jnp.bfloat16)
            chosen = jnp.concatenate([chosen] * 3, axis=0)
            picked = jnp.dot(table, chosen, preferred_element_type=jnp.float32)
            here = places == ins[left : left + 1, span]
            return [
                jnp.sum(
                    jnp.where(here, picked[part * inserts : (part + 1) * inserts], 0.0),
                    axis=0,
                    keepdims=True,
                )
                for part in range(2 * pairs)
            ]

        first, second = values(0, 1), values(2, 3)
        scale = coef[:, span]
        sums = [jnp.zeros((1, step), jnp.float32) for _ in range(8)]
        for pair in range(pairs):
            a, b = first[2 * pair], first[2 * pair + 1]
            c, d = second[2 * pair], second[2 * pair + 1]
            real, imag = scale * (a * c - b * d), scale * (a * d + b * c)
            for apart in range(3):
                sums[2 * apart] += weight[3 * pair + apart] * real
                sums[2 * apart + 1] += weight[3 * pair + apart] * imag
        rows = thirds(jnp.concatenate(sums, axis=0), 0)
        bins = lax.broadcasted_iota(jnp.int32, (entries, step), 0)
        bins = (bins == entry[:, span]).astype(jnp.bfloat16)
        spread = nt_dot(rows, bins)
        total += spread[:8] + spread[8:16] + spread[16:]
    out[...] = total


def direct(grams, swap, weight, ins, coef, entry, entries):
    size = grams[0].shape[0]
    smem = pl.BlockSpec(memory_space=pltpu.SMEM)
    vmem = pl.BlockSpec(memory_space=pltpu.VMEM)
    return pl.pallas_call(
        direct_kernel,
        in_specs=[smem, smem] + [vmem] * (3 + len(grams)),
        out_specs=vmem,
        out_shape=jax.ShapeDtypeStruct((8, entries), jnp.float32),
        scratch_shapes=[pltpu.VMEM((len(grams) * size, size // 2), jnp.float32)],
        name="direct",
    )(swap, weight, ins, coef, entry, *grams)


def after(value, *others):
    return lax.optimization_barrier((value,) + others)[0]


def total_over(value, axis):
    devices = lax.axis_size(axis)
    if devices & (devices - 1):
        return lax.psum(value, axis)
    distance = 1
    while distance < devices:
        value = value + lax.ppermute(value, axis, [(i, i ^ distance) for i in range(devices)])
        distance *= 2
    return value


def local(
    meson_fields, perambulators, direct_ins, direct_coef, direct_entry, box_ins, box_coef, box_entry
):
    devices = lax.axis_size("tm")
    owned = 4
    entries = owned * devices
    here = lax.axis_index("tm")
    role = here % GROUP
    everyone = range(devices)

    def move(value, target):
        route = [(i, target[i % GROUP](i) % devices) for i in everyone if i % GROUP in target]
        return lax.ppermute(value, "tm", route)

    def by_role(*choices):
        picked = jnp.asarray(choices[3])
        for number in range(3):
            picked = jnp.where(role == number, choices[number], picked)
        return picked

    fields = meson_fields[:, :, 0]
    factor = perambulators[:, 0]
    own = [dress(fields, factor, chunk) for chunk in range(CHUNKS)]
    half = CHUNKS // 2

    across = {0: lambda i: i + 1, 1: lambda i: i + 2, 2: lambda i: i - 2, 3: lambda i: i - 1}
    along = {0: lambda i: i - GROUP, 3: lambda i: i + GROUP}
    beside = {0: lambda i: i + 1, 3: lambda i: i - 1}
    cross = {0: lambda i: i + 2, 3: lambda i: i - 2}

    terms = box_ins.shape[0]
    ins_table = box_ins.T
    swapped_table = ins_table[jnp.array([1, 0, 3, 2])]
    part = terms // 2
    late_table = jnp.where(role == 1, ins_table[:, part:], swapped_table[:, :part])
    send_table = jnp.where(role == 0, swapped_table[:, :part], ins_table[:, part:])
    late_entry = jnp.where(role == 1, box_entry[part:], box_entry[:part])
    late_coef = jnp.where(role == 1, box_coef[part:], box_coef[:part])

    near = [None] * CHUNKS
    near[0] = move(own[0], across)
    split = [jnp.where(role == 0, own[half + j], own[j]) for j in range(half)]
    chosen = jnp.concatenate([send_table[0], send_table[2]])
    extra = pick(own, chosen, jnp.where(role == 0, 0, 1).astype(jnp.int32)[None])
    far = [move(own[chunk], along) for chunk in range(CHUNKS)]
    split_in = [None] * half
    split_in[0] = move(split[0], cross)
    split_in[1] = move(after(split[1], near[0]), cross)
    near[1] = move(after(own[1], split_in[0]), across)
    extra_in = move(after(extra, split_in[0]), cross)
    near[2] = move(after(own[2], split_in[1]), across)
    near[3] = move(after(own[3], near[1]), across)

    far_beside = [move(far[chunk], beside) for chunk in range(CHUNKS)]
    near_beside = [move(near[chunk], beside) for chunk in range(CHUNKS)]

    edge = (role == 0) | (role == 3)

    tables = [
        lax.cond(
            edge,
            lambda o, a, z, c: gram([o, a, z], 2),
            lambda o, a, z, c: gram([o, a, c], 2),
            own[chunk],
            near[chunk],
            far[chunk],
            near_beside[chunk],
        )
        for chunk in range(CHUNKS)
    ]
    table = functools.reduce(lambda a, b: a + b, tables)
    size = 2 * fields.shape[1]
    same_gram = table[:size, :size]
    near_gram = table[:size, size : 2 * size]
    third_gram = jnp.where(edge, table[size:, 2 * size :], table[:size, 2 * size :])

    split_gram = functools.reduce(
        lambda a, b: a + b,
        [
            lax.cond(
                role == 1,
                lambda v, lo, hi: gram([v, lo], 1),
                lambda v, lo, hi: gram([v, hi], 1),
                split_in[j],
                far_beside[j],
                far_beside[half + j],
            )
            for j in range(half)
        ],
    )[:, size:]
    split_other = move(split_gram, {2: lambda i: i - 5})
    split_gram = split_gram + split_other.T

    one = jnp.float32(1.0)
    zero = jnp.float32(0.0)

    def weights(first, second, third):
        return jnp.stack([first + zero, second + zero, third + zero])

    outer = jnp.where(edge, one, zero)
    inner = one - outer
    same_weight = weights(one, zero, zero)
    near_weight = weights(zero, inner, outer)
    third_weight = weights(zero, by_role(zero, zero, one, zero), outer)
    split_weight = weights(zero, by_role(zero, one, zero, zero), zero)
    near_swap = by_role(0, 1, 0, 1)
    third_swap = by_role(0, 0, 1, 1)
    split_swap = jnp.int32(0)
    direct_sum = direct(
        [same_gram, near_gram, third_gram, split_gram],
        jnp.stack([jnp.int32(0), near_swap, third_swap, split_swap]),
        jnp.concatenate([same_weight, near_weight, third_weight, split_weight]),
        direct_ins.T,
        direct_coef[None],
        direct_entry[None],
        entries,
    )

    def with_sign(weight, swap):
        return jnp.concatenate([weight, jnp.where(swap == 1, -one, one)[None]])

    def role_table(swap):
        return jnp.where(swap == 1, swapped_table, ins_table)

    same_box = box(
        own, own, ins_table, box_entry, box_coef, with_sign(same_weight, 0), entries
    )
    near_box = box(
        own, near, role_table(near_swap), box_entry, box_coef,
        with_sign(near_weight, near_swap), entries,
    )
    third_box = lax.cond(
        edge,
        lambda o, a, z, c, t, e, k, w: box(a, z, t, e, k, w, entries),
        lambda o, a, z, c, t, e, k, w: box(o, c, t, e, k, w, entries),
        own, near, far, near_beside, role_table(third_swap), box_entry, box_coef,
        with_sign(third_weight, third_swap),
    )
    extras = [extra_in[j] for j in range(half)]
    both_inner = weights(zero, inner, zero)
    split_box = lax.cond(
        role == 1,
        lambda v, x, f, t, e, k, w: box(v + x, f, t, e, k, w, entries, slots=half),
        lambda v, x, f, t, e, k, w: box(
            v + x, f[half:] + f[:half], t, e, k, w, entries, slots=half
        ),
        split_in, extras, far_beside, late_table, late_entry, late_coef,
        with_sign(both_inner, by_role(0, 0, 1, 0)),
    )
    partial = direct_sum - (same_box + near_box + third_box + split_box)
    summed = total_over(partial, "tm") / devices
    mine = lax.dynamic_slice_in_dim(summed[:6], here * owned, owned, axis=1)
    return mine.reshape(3, 2, owned)


def solution(mesh):
    placed = (
        P(None, None, ("cfg", "tm"), None, None),
        P(None, ("cfg", "tm"), None, None),
        P(),
        P(),
        P(),
        P(),
        P(),
        P(),
    )
    return jax.shard_map(
        local, mesh=mesh, in_specs=placed, out_specs=P(None, None, ("cfg", "tm")), check_vma=False
    )
```

```python
import functools

import jax
import jax.numpy as jnp
from jax import lax
from jax.experimental import pallas as pl
from jax.experimental.pallas import tpu as pltpu
from jax.sharding import PartitionSpec as P

CHUNKS = 4
GROUP = 4
STEP_ROWS = 16
STEP_INS = 8
TERM_STEP = 512
NT = (((1,), (1,)), ((), ()))


def nt_dot(left, right):
    return lax.dot_general(left, right, NT, preferred_element_type=jnp.float32)


def dress_kernel(fields, factor, *refs):
    outs, weight = refs[:-1], refs[-1]
    modes = factor.shape[-1]
    step = pl.program_id(0)

    @pl.when(step == 0)
    def _():
        weight[:modes, :modes] = factor[0]
        weight[:modes, modes:] = factor[1]
        weight[modes:, :modes] = -factor[1]
        weight[modes:, modes:] = factor[0]

    inserts, rows = fields.shape[1:3]
    sides = fields[...].reshape(2, inserts * rows, modes)
    product = jnp.dot(
        jnp.concatenate([sides[0], sides[1]], axis=1),
        weight[...],
        preferred_element_type=jnp.float32,
    )
    steps = pl.num_programs(0) // len(outs)
    for number, out in enumerate(outs):

        @pl.when(step // steps == number)
        def _(out=out):
            out[0] = product[:, :modes].reshape(inserts, rows, modes).astype(out.dtype)
            out[1] = product[:, modes:].reshape(inserts, rows, modes).astype(out.dtype)


def dress(fields, factor, first, count):
    inserts, modes = fields.shape[1], fields.shape[-1]
    rows = modes // CHUNKS
    steps = inserts // STEP_INS
    block = (2, STEP_INS, rows, modes)

    def place(number):
        return lambda g: (0, jnp.clip(g - number * steps, 0, steps - 1), 0, 0)

    return pl.pallas_call(
        dress_kernel,
        grid=(count * steps,),
        in_specs=[
            pl.BlockSpec(block, lambda g: (0, g % steps, first + g // steps, 0)),
            pl.BlockSpec((2, modes, modes), lambda g: (0, 0, 0)),
        ],
        out_specs=[pl.BlockSpec(block, place(number)) for number in range(count)],
        out_shape=[jax.ShapeDtypeStruct((2, inserts, rows, modes), fields.dtype)] * count,
        scratch_shapes=[pltpu.VMEM((2 * modes, 2 * modes), fields.dtype)],
        cost_estimate=pl.CostEstimate(
            flops=16 * count * inserts * rows * modes * modes,
            bytes_accessed=8 * count * inserts * rows * modes,
            transcendentals=0,
        ),
        name="dress",
    )(fields, factor)


def gram_kernel(count, left_count, *refs):
    blocks, before, out, flat = refs[:count], refs[count], refs[count + 1], refs[count + 2]
    _, inserts, rows, modes = blocks[0].shape
    size = 2 * inserts
    for index, block in enumerate(blocks):
        flat[index * size : (index + 1) * size] = block[...].reshape(size, rows * modes)
    product = nt_dot(flat[: left_count * size], flat[(count - out.shape[1] // size) * size :])

    @pl.when(pl.program_id(0) == 0)
    def _():
        out[...] = before[...] + product

    @pl.when(pl.program_id(0) > 0)
    def _():
        out[...] += product


def gram(blocks, left_count, right_count, before):
    count = len(blocks)
    _, inserts, rows, modes = blocks[0].shape
    size = 2 * inserts
    spec = pl.BlockSpec((2, inserts, STEP_ROWS, modes), lambda i: (0, 0, i, 0))
    shape = (left_count * size, right_count * size)
    whole = pl.BlockSpec(shape, lambda i: (0, 0))
    return pl.pallas_call(
        functools.partial(gram_kernel, count, left_count),
        grid=(rows // STEP_ROWS,),
        in_specs=[spec] * count + [whole],
        out_specs=whole,
        out_shape=jax.ShapeDtypeStruct(shape, jnp.float32),
        scratch_shapes=[pltpu.VMEM((count * size, STEP_ROWS * modes), jnp.bfloat16)],
        cost_estimate=pl.CostEstimate(
            flops=16 * shape[0] * shape[1] * rows * modes,
            bytes_accessed=count * 2 * size * rows * modes,
            transcendentals=0,
        ),
        name="gram",
    )(*blocks, before)


def box_kernel(left_count, right_count, ins, entry, coef, weight, before, *refs):
    left, refs = refs[:left_count], refs[left_count:]
    right, refs = refs[:right_count], refs[right_count:]
    extra, (out, held, sems) = refs[:-3], refs[-3:]
    terms = held.shape[0]
    rows = left[0].shape[2]

    @pl.loop(0, terms)
    def _(term):
        for place in range(4):
            where = ins[place, term]
            sources = [ref.at[:, where] for ref in (right if place % 2 else left)]
            if place % 2 == 0:
                for ref in extra:
                    where = (place // 2) * terms + term
                    sources += [ref.at[number, :, where] for number in range(ref.shape[0])]
            for number, source in enumerate(sources):
                pltpu.make_async_copy(
                    source,
                    held.at[term, place, :, pl.ds(number * rows, rows)],
                    sems.at[term],
                ).start()

    def product(term, one, other):
        real, imag = held[term, one, 0], held[term, one, 1]
        other_side = jnp.concatenate([held[term, other, 0], held[term, other, 1]], axis=1)
        return (
            nt_dot(jnp.concatenate([real, imag], axis=1), other_side),
            nt_dot(jnp.concatenate([imag, -real], axis=1), other_side),
        )

    out[...] = before[...]
    spot = lax.broadcasted_iota(jnp.int32, out.shape, 1)
    line = lax.broadcasted_iota(jnp.int32, out.shape, 0)

    @pl.loop(0, terms)
    def _(term):
        pltpu.make_async_copy(held.at[term], held.at[term], sems.at[term]).wait()
        first_real, first_imag = product(term, 0, 1)
        second_real, second_imag = product(term, 3, 2)
        real = jnp.sum(first_real * second_real + first_imag * second_imag) * coef[term]
        imag = jnp.sum(first_imag * second_real - first_real * second_imag) * coef[term]
        imag = imag * weight[3]
        added = jnp.zeros(out.shape, jnp.float32)
        for apart in range(3):
            added = jnp.where(line == 2 * apart, real * weight[apart], added)
            added = jnp.where(line == 2 * apart + 1, imag * weight[apart], added)
        out[...] -= jnp.where(spot == entry[term], added, 0.0)


def box(left, right, ins, entry, coef, weight, before, extra=None):
    extra = [] if extra is None else [extra]
    terms = ins.shape[1]
    modes = left[0].shape[3]
    count = len(left) + len(right) + len(extra)
    smem = pl.BlockSpec(memory_space=pltpu.SMEM)
    vmem = pl.BlockSpec(memory_space=pltpu.VMEM)
    return pl.pallas_call(
        functools.partial(box_kernel, len(left), len(right)),
        in_specs=[smem] * 4 + [vmem] + [pl.BlockSpec(memory_space=pl.ANY)] * count,
        out_specs=vmem,
        out_shape=jax.ShapeDtypeStruct(before.shape, jnp.float32),
        scratch_shapes=[
            pltpu.VMEM((terms, 4, 2, modes, modes), left[0].dtype),
            pltpu.SemaphoreType.DMA((terms,)),
        ],
        cost_estimate=pl.CostEstimate(
            flops=32 * terms * modes * modes * modes,
            bytes_accessed=16 * terms * modes * modes,
            transcendentals=0,
        ),
        name="box",
    )(ins, entry, coef, weight, before, *left, *right, *extra)


def pick_kernel(upper, ins, *refs):
    del ins
    blocks, out = refs[:-1], refs[-1]
    half = len(blocks) // 2

    @pl.when(upper[0] == 1)
    def _():
        for number in range(half):
            out[number] = blocks[half + number][...]

    @pl.when(upper[0] == 0)
    def _():
        for number in range(half):
            out[number] = blocks[number][...]


def pick(blocks, places, upper):
    _, _, rows, modes = blocks[0].shape
    half, count = len(blocks) // 2, places.shape[0]
    spec = pl.BlockSpec((2, 1, rows, modes), lambda l, upper, ins: (0, ins[l], 0, 0))
    return pl.pallas_call(
        pick_kernel,
        grid_spec=pltpu.PrefetchScalarGridSpec(
            num_scalar_prefetch=2,
            grid=(count,),
            in_specs=[spec] * len(blocks),
            out_specs=pl.BlockSpec(
                (half, 2, 1, rows, modes), lambda l, upper, ins: (0, 0, l, 0, 0)
            ),
        ),
        out_shape=jax.ShapeDtypeStruct((half, 2, count, rows, modes), blocks[0].dtype),
        name="pick",
    )(upper, places, *blocks)


def thirds(value, axis):
    high = value.astype(jnp.bfloat16)
    rest = value - high.astype(jnp.float32)
    middle = rest.astype(jnp.bfloat16)
    low = (rest - middle.astype(jnp.float32)).astype(jnp.bfloat16)
    return jnp.concatenate([high, middle, low], axis=axis)


def direct_kernel(swap, weight, ins, coef, entry, before, *refs):
    tables, out, lines = refs[:-2], refs[-2], refs[-1]
    size = 2 * lines.shape[1]
    inserts = size // 2
    if len(tables) == 1:
        grams = [tables[0][:size, place * size : (place + 1) * size] for place in range(3)]
        below = tables[0][size:, 2 * size :]
        grams[2] = jnp.where(swap[3] == 1, below, grams[2])
    else:
        grams = [tables[0][...] + tables[1][...].T]
    pairs = len(grams)
    for pair, table in enumerate(grams):
        table = jnp.where(swap[pair] == 1, table.T, table)
        upper, lower = table[:inserts], table[inserts:]
        lines[pair * size : pair * size + inserts] = upper[:, :inserts] + lower[:, inserts:]
        lines[pair * size + inserts : (pair + 1) * size] = lower[:, :inserts] - upper[:, inserts:]
    table = thirds(lines[...], 1)
    entries = out.shape[1]
    total = before[...]
    step = min(TERM_STEP, ins.shape[1])
    for start in range(0, ins.shape[1], step):
        span = slice(start, start + step)
        places = lax.broadcasted_iota(jnp.int32, (inserts, step), 0)

        def values(left, right):
            chosen = (places == ins[right : right + 1, span]).astype(jnp.bfloat16)
            chosen = jnp.concatenate([chosen] * 3, axis=0)
            picked = jnp.dot(table, chosen, preferred_element_type=jnp.float32)
            here = places == ins[left : left + 1, span]
            return [
                jnp.sum(
                    jnp.where(here, picked[part * inserts : (part + 1) * inserts], 0.0),
                    axis=0,
                    keepdims=True,
                )
                for part in range(2 * pairs)
            ]

        first, second = values(0, 1), values(2, 3)
        scale = coef[:, span]
        sums = [jnp.zeros((1, step), jnp.float32) for _ in range(8)]
        for pair in range(pairs):
            a, b = first[2 * pair], first[2 * pair + 1]
            c, d = second[2 * pair], second[2 * pair + 1]
            real, imag = scale * (a * c - b * d), scale * (a * d + b * c)
            for apart in range(3):
                sums[2 * apart] += weight[3 * pair + apart] * real
                sums[2 * apart + 1] += weight[3 * pair + apart] * imag
        rows = thirds(jnp.concatenate(sums, axis=0), 0)
        bins = lax.broadcasted_iota(jnp.int32, (entries, step), 0)
        bins = (bins == entry[:, span]).astype(jnp.bfloat16)
        spread = nt_dot(rows, bins)
        total += spread[:8] + spread[8:16] + spread[16:]
    out[...] = total


def direct(tables, pairs, swap, weight, ins, coef, entry, before):
    size = tables[0].shape[0] // (2 if pairs == 3 else 1)
    smem = pl.BlockSpec(memory_space=pltpu.SMEM)
    vmem = pl.BlockSpec(memory_space=pltpu.VMEM)
    return pl.pallas_call(
        direct_kernel,
        in_specs=[smem, smem] + [vmem] * (4 + len(tables)),
        out_specs=vmem,
        out_shape=jax.ShapeDtypeStruct(before.shape, jnp.float32),
        scratch_shapes=[pltpu.VMEM((pairs * size, size // 2), jnp.float32)],
        cost_estimate=pl.CostEstimate(
            flops=2 * pairs * size * size * ins.shape[1] * 3,
            bytes_accessed=40 * ins.shape[1],
            transcendentals=0,
        ),
        name="direct",
    )(swap, weight, ins, coef, entry, before, *tables)


def after(value, *others):
    return lax.optimization_barrier((value,) + others)[0]


def total_over(value, axis):
    devices = lax.axis_size(axis)
    if devices & (devices - 1):
        return lax.psum(value, axis)
    distance = 1
    while distance < devices:
        value = value + lax.ppermute(value, axis, [(i, i ^ distance) for i in range(devices)])
        distance *= 2
    return value


def local(
    meson_fields, perambulators, direct_ins, direct_coef, direct_entry, box_ins, box_coef, box_entry
):
    devices = lax.axis_size("tm")
    owned = 4
    entries = owned * devices
    here = lax.axis_index("tm")
    role = here % GROUP
    everyone = range(devices)

    def move(value, target):
        route = [(i, target[i % GROUP](i) % devices) for i in everyone if i % GROUP in target]
        return lax.ppermute(value, "tm", route)

    def by_role(*choices):
        picked = jnp.asarray(choices[3])
        for number in range(3):
            picked = jnp.where(role == number, choices[number], picked)
        return picked

    fields = meson_fields[:, :, 0]
    factor = perambulators[:, 0]
    own = dress(fields, factor, 0, 1) + dress(fields, factor, 1, CHUNKS - 1)
    half = CHUNKS // 2

    across = {0: lambda i: i + 1, 1: lambda i: i + 2, 2: lambda i: i - 2, 3: lambda i: i - 1}
    along = {0: lambda i: i - GROUP, 3: lambda i: i + GROUP}
    beside = {0: lambda i: i + 1, 3: lambda i: i - 1}
    cross = {0: lambda i: i + 2, 3: lambda i: i - 2}

    terms = box_ins.shape[0]
    ins_table = box_ins.T
    swapped_table = ins_table[jnp.array([1, 0, 3, 2])]
    part = terms // 2
    late_table = jnp.where(role == 1, ins_table[:, part:], swapped_table[:, :part])
    send_table = jnp.where(role == 0, swapped_table[:, :part], ins_table[:, part:])
    late_entry = jnp.where(role == 1, box_entry[part:], box_entry[:part])
    late_coef = jnp.where(role == 1, box_coef[part:], box_coef[:part])

    near, far = [], []
    for chunk in range(CHUNKS):
        near.append(move(own[chunk], across))
        far.append(move(own[chunk], along))
    split = [jnp.where(role == 0, own[half + j], own[j]) for j in range(half)]
    chosen = jnp.concatenate([send_table[0], send_table[2]])
    extra = pick(own, chosen, jnp.where(role == 0, 0, 1).astype(jnp.int32)[None])
    split_in = []
    for piece in split:
        split_in.append(move(after(piece, near[CHUNKS - 2]), cross))
    extra_in = move(after(extra, near[CHUNKS - 2]), cross)

    edge = (role == 0) | (role == 3)
    one, zero = jnp.float32(1.0), jnp.float32(0.0)

    def weights(first, second, third):
        return jnp.stack([first + zero, second + zero, third + zero])

    def with_sign(weight, swap):
        return jnp.concatenate([weight, jnp.where(swap == 1, -one, one)[None]])

    def role_table(swap):
        return jnp.where(swap == 1, swapped_table, ins_table)

    outer = jnp.where(edge, one, zero)
    inner = one - outer
    same_weight = weights(one, zero, zero)
    near_weight = weights(zero, inner, outer)
    third_weight = weights(zero, by_role(zero, zero, one, zero), outer)
    split_weight = weights(zero, by_role(zero, one, zero, zero), zero)
    both_inner = weights(zero, inner, zero)
    near_swap = by_role(0, 1, 0, 1)
    third_swap = by_role(0, 0, 1, 1)
    size = 2 * fields.shape[1]

    total = box(
        own, own, ins_table, box_entry, box_coef, with_sign(same_weight, 0),
        jnp.zeros((8, entries), jnp.float32),
    )
    table = jnp.zeros((2 * size, 3 * size), jnp.float32)
    early = (total, extra) + tuple(split)
    near_beside = []
    for chunk in range(CHUNKS):
        near_beside.append(move(after(near[chunk], *early), beside))
        table = lax.cond(
            edge,
            lambda o, a, z, c, t: gram([o, a, z], 2, 3, t),
            lambda o, a, z, c, t: gram([o, a, c], 2, 3, t),
            own[chunk], near[chunk], far[chunk], near_beside[chunk], table,
        )
        early = (table,)
    far_beside = [move(after(piece, table), beside) for piece in far]
    total = after(total, table)
    total = box(
        own, near, role_table(near_swap), box_entry, box_coef,
        with_sign(near_weight, near_swap), total,
    )
    total = lax.cond(
        edge,
        lambda o, a, z, c, *rest: box(a, z, *rest),
        lambda o, a, z, c, *rest: box(o, c, *rest),
        own, near, far, near_beside, role_table(third_swap), box_entry, box_coef,
        with_sign(third_weight, third_swap), total,
    )
    direct_table = direct_ins.T
    total = direct(
        [table], 3,
        jnp.stack([jnp.int32(0), near_swap, third_swap, edge.astype(jnp.int32)]),
        jnp.concatenate([same_weight, near_weight, third_weight]),
        direct_table, direct_coef[None], direct_entry[None], total,
    )
    split_gram = after(jnp.zeros((size, size), jnp.float32), total)
    for j in range(half):
        split_gram = lax.cond(
            role == 1,
            lambda v, lo, hi, t: gram([v, lo], 1, 1, t),
            lambda v, lo, hi, t: gram([v, hi], 1, 1, t),
            split_in[j], far_beside[j], far_beside[half + j], split_gram,
        )
    split_other = move(split_gram, {2: lambda i: i - 5})
    total = direct(
        [split_gram, split_other], 1, jnp.zeros((4,), jnp.int32), split_weight,
        direct_table, direct_coef[None], direct_entry[None], total,
    )
    total = lax.cond(
        role == 1,
        lambda v, x, f, *rest: box(v, f, *rest, extra=x),
        lambda v, x, f, *rest: box(v, f[half:] + f[:half], *rest, extra=x),
        split_in, extra_in, far_beside, late_table, late_entry, late_coef,
        with_sign(both_inner, by_role(0, 0, 1, 0)), total,
    )
    summed = total_over(total, "tm") / devices
    mine = lax.dynamic_slice_in_dim(summed[:6], here * owned, owned, axis=1)
    return mine.reshape(3, 2, owned)


def solution(mesh):
    placed = (
        P(None, None, ("cfg", "tm"), None, None),
        P(None, ("cfg", "tm"), None, None),
        P(),
        P(),
        P(),
        P(),
        P(),
        P(),
    )

    return jax.shard_map(
        local, mesh=mesh, in_specs=placed, out_specs=P(None, None, ("cfg", "tm")), check_vma=False
    )
```

```python
import functools

import jax
import jax.numpy as jnp
from jax import lax
from jax.experimental import pallas as pl
from jax.experimental.pallas import tpu as pltpu
from jax.sharding import PartitionSpec as P

PARTS = (1, 1, 1, 1)
GROUP = 4
STEP_ROWS = 16
STEP_INS = 8
TERM_STEP = 512
NT = (((1,), (1,)), ((), ()))


def nt_dot(left, right):
    return lax.dot_general(left, right, NT, preferred_element_type=jnp.float32)


def dress_kernel(out_steps, fields, factor, *refs):
    outs, weight = refs[:-1], refs[-1]
    modes = factor.shape[-1]
    step = pl.program_id(0)

    @pl.when(step == 0)
    def _():
        weight[:modes, :modes] = factor[0]
        weight[:modes, modes:] = factor[1]
        weight[modes:, :modes] = -factor[1]
        weight[modes:, modes:] = factor[0]

    inserts, rows = fields.shape[1:3]
    sides = fields[...].reshape(2, inserts * rows, modes)
    product = jnp.dot(
        jnp.concatenate([sides[0], sides[1]], axis=1),
        weight[...],
        preferred_element_type=jnp.float32,
    )
    first = 0
    for out, count in zip(outs, out_steps):

        @pl.when((step >= first) & (step < first + count))
        def _(out=out):
            out[0] = product[:, :modes].reshape(inserts, rows, modes).astype(out.dtype)
            out[1] = product[:, modes:].reshape(inserts, rows, modes).astype(out.dtype)

        first += count


def dress(fields, factor, first, parts):
    inserts, modes = fields.shape[1], fields.shape[-1]
    rows = modes // sum(PARTS)
    steps = inserts // STEP_INS
    block = (2, STEP_INS, rows, modes)
    total = sum(parts)

    def place(before, part):
        def where(g):
            own = jnp.clip(g - before * steps, 0, part * steps - 1)
            return 0, own % steps, own // steps, 0

        return where

    return pl.pallas_call(
        functools.partial(dress_kernel, [part * steps for part in parts]),
        grid=(total * steps,),
        in_specs=[
            pl.BlockSpec(block, lambda g: (0, g % steps, first + g // steps, 0)),
            pl.BlockSpec((2, modes, modes), lambda g: (0, 0, 0)),
        ],
        out_specs=[
            pl.BlockSpec(block, place(sum(parts[:number]), part))
            for number, part in enumerate(parts)
        ],
        out_shape=[
            jax.ShapeDtypeStruct((2, inserts, part * rows, modes), fields.dtype) for part in parts
        ],
        scratch_shapes=[pltpu.VMEM((2 * modes, 2 * modes), fields.dtype)],
        cost_estimate=pl.CostEstimate(
            flops=16 * total * inserts * rows * modes * modes,
            bytes_accessed=8 * total * inserts * rows * modes,
            transcendentals=0,
        ),
        name="dress",
    )(fields, factor)


def gram_kernel(count, left_count, *refs):
    blocks, before, out, flat = refs[:count], refs[count], refs[count + 1], refs[count + 2]
    _, inserts, rows, modes = blocks[0].shape
    size = 2 * inserts
    for index, block in enumerate(blocks):
        flat[index * size : (index + 1) * size] = block[...].reshape(size, rows * modes)
    product = nt_dot(flat[: left_count * size], flat[(count - out.shape[1] // size) * size :])

    @pl.when(pl.program_id(0) == 0)
    def _():
        out[...] = before[...] + product

    @pl.when(pl.program_id(0) > 0)
    def _():
        out[...] += product


def gram(blocks, left_count, right_count, before, offset=0):
    count = len(blocks)
    _, inserts, rows, modes = blocks[0].shape
    size = 2 * inserts
    block = (2, inserts, STEP_ROWS, modes)
    spec = pl.BlockSpec(block, lambda i: (0, 0, i, 0))
    last = pl.BlockSpec(block, lambda i: (0, 0, offset // STEP_ROWS + i, 0))
    shape = (left_count * size, right_count * size)
    whole = pl.BlockSpec(shape, lambda i: (0, 0))
    return pl.pallas_call(
        functools.partial(gram_kernel, count, left_count),
        grid=(rows // STEP_ROWS,),
        in_specs=[spec] * (count - 1) + [last, whole],
        out_specs=whole,
        out_shape=jax.ShapeDtypeStruct(shape, jnp.float32),
        scratch_shapes=[pltpu.VMEM((count * size, STEP_ROWS * modes), jnp.bfloat16)],
        cost_estimate=pl.CostEstimate(
            flops=16 * shape[0] * shape[1] * rows * modes,
            bytes_accessed=count * 2 * size * rows * modes,
            transcendentals=0,
        ),
        name="gram",
    )(*blocks, before)


def box_kernel(counts, ins, scale, before, *refs):
    groups = []
    for left_count, right_count, extra_count in counts:
        left, refs = refs[:left_count], refs[left_count:]
        right, refs = refs[:right_count], refs[right_count:]
        extra, refs = refs[:extra_count], refs[extra_count:]
        groups.append((left, right, extra))
    out, held, sems = refs
    terms = held.shape[0] // len(groups)

    def fetch(group, term):
        left, right, extra = groups[group]
        slot = group * terms + term
        for place in range(4):
            where = ins[place, slot]
            sources = [ref.at[:, where] for ref in (right if place % 2 else left)]
            if place % 2 == 0:
                for ref in extra:
                    where = (place // 2) * terms + term
                    sources += [ref.at[number, :, where] for number in range(ref.shape[0])]
            start = 0
            for source in sources:
                rows = source.shape[1]
                pltpu.make_async_copy(
                    source, held.at[slot, place, :, pl.ds(start, rows)], sems.at[slot]
                ).start()
                start += rows

    @pl.loop(0, terms)
    def _(term):
        fetch(0, term)

    def product(slot, one, other):
        real, imag = held[slot, one, 0], held[slot, one, 1]
        other_side = jnp.concatenate([held[slot, other, 0], held[slot, other, 1]], axis=1)
        return (
            nt_dot(jnp.concatenate([real, imag], axis=1), other_side),
            nt_dot(jnp.concatenate([imag, -real], axis=1), other_side),
        )

    out[...] = before[...]
    spot = lax.broadcasted_iota(jnp.int32, out.shape, 1)
    line = lax.broadcasted_iota(jnp.int32, out.shape, 0)
    for group in range(len(groups)):

        @pl.loop(0, terms)
        def _(term, group=group):
            if group + 1 < len(groups):
                fetch(group + 1, term)
            slot = group * terms + term
            pltpu.make_async_copy(held.at[slot], held.at[slot], sems.at[slot]).wait()
            first_real, first_imag = product(slot, 0, 1)
            second_real, second_imag = product(slot, 3, 2)
            real = jnp.sum(first_real * second_real + first_imag * second_imag)
            imag = jnp.sum(first_imag * second_real - first_real * second_imag)
            imag = imag * scale[3, slot]
            added = jnp.zeros(out.shape, jnp.float32)
            for apart in range(3):
                added = jnp.where(line == 2 * apart, real * scale[apart, slot], added)
                added = jnp.where(line == 2 * apart + 1, imag * scale[apart, slot], added)
            out[...] -= jnp.where(spot == ins[4, slot], added, 0.0)


def box(groups, table, before):
    ins, scale = table
    slots = ins.shape[1]
    modes = groups[0][0][0].shape[3]
    kind = groups[0][0][0].dtype
    arrays = [ref for group in groups for refs in group for ref in refs]
    smem = pl.BlockSpec(memory_space=pltpu.SMEM)
    vmem = pl.BlockSpec(memory_space=pltpu.VMEM)
    return pl.pallas_call(
        functools.partial(box_kernel, [tuple(len(refs) for refs in group) for group in groups]),
        in_specs=[smem, smem, vmem] + [pl.BlockSpec(memory_space=pl.ANY)] * len(arrays),
        out_specs=vmem,
        out_shape=jax.ShapeDtypeStruct(before.shape, jnp.float32),
        scratch_shapes=[
            pltpu.VMEM((slots, 4, 2, modes, modes), kind),
            pltpu.SemaphoreType.DMA((slots,)),
        ],
        cost_estimate=pl.CostEstimate(
            flops=32 * slots * modes * modes * modes,
            bytes_accessed=16 * slots * modes * modes,
            transcendentals=0,
        ),
        name="box",
    )(ins, scale, before, *arrays)


def pick_kernel(count, upper, places, *refs):
    blocks, outs, (held, sems) = refs[:count], refs[count:-2], refs[-2:]
    terms = places.shape[0]

    def fetch(term):
        def go(sources, start=0):
            for source in sources:
                pltpu.make_async_copy(
                    source, held.at[term, :, pl.ds(start, source.shape[1])], sems.at[term]
                ).start()
                start += source.shape[1]

        where = places[term]

        @pl.when(upper[0] == 1)
        def _():
            go([ref.at[:, where] for ref in blocks[count // 2 :]])

        @pl.when(upper[0] == 0)
        def _():
            go([ref.at[:, where] for ref in blocks[: count // 2]])

    for term in range(terms):
        fetch(term)
    share = terms // len(outs)
    for term in range(terms):
        pltpu.make_async_copy(held.at[term], held.at[term], sems.at[term]).wait()
        target = outs[term // share].at[0, :, term % share]
        pltpu.make_async_copy(held.at[term], target, sems.at[term]).start()
    for term in range(terms):
        target = outs[term // share].at[0, :, term % share]
        pltpu.make_async_copy(held.at[term], target, sems.at[term]).wait()


def pick(blocks, places, upper, shares):
    modes = blocks[0].shape[3]
    rows = modes // 2
    count = places.shape[0]
    smem = pl.BlockSpec(memory_space=pltpu.SMEM)
    hbm = pl.BlockSpec(memory_space=pl.ANY)
    return pl.pallas_call(
        functools.partial(pick_kernel, len(blocks)),
        in_specs=[smem, smem] + [hbm] * len(blocks),
        out_specs=[hbm] * shares,
        out_shape=[
            jax.ShapeDtypeStruct((1, 2, count // shares, rows, modes), blocks[0].dtype)
        ] * shares,
        scratch_shapes=[
            pltpu.VMEM((count, 2, rows, modes), blocks[0].dtype),
            pltpu.SemaphoreType.DMA((count,)),
        ],
        cost_estimate=pl.CostEstimate(
            flops=0, bytes_accessed=8 * count * rows * modes, transcendentals=0
        ),
        name="pick",
    )(upper, places, *blocks)


def thirds(value, axis):
    high = value.astype(jnp.bfloat16)
    rest = value - high.astype(jnp.float32)
    middle = rest.astype(jnp.bfloat16)
    low = (rest - middle.astype(jnp.float32)).astype(jnp.bfloat16)
    return jnp.concatenate([high, middle, low], axis=axis)


def direct_kernel(swap, weight, ins, coef, entry, before, *refs):
    tables, out, lines = refs[:-2], refs[-2], refs[-1]
    size = 2 * lines.shape[1]
    inserts = size // 2
    if len(tables) == 1:
        grams = [tables[0][:size, place * size : (place + 1) * size] for place in range(3)]
        below = tables[0][size:, 2 * size :]
        grams[2] = jnp.where(swap[3] == 1, below, grams[2])
    else:
        grams = [tables[0][...] + tables[1][...].T]
    pairs = len(grams)
    for pair, table in enumerate(grams):
        table = jnp.where(swap[pair] == 1, table.T, table)
        upper, lower = table[:inserts], table[inserts:]
        lines[pair * size : pair * size + inserts] = upper[:, :inserts] + lower[:, inserts:]
        lines[pair * size + inserts : (pair + 1) * size] = lower[:, :inserts] - upper[:, inserts:]
    table = thirds(lines[...], 1)
    entries = out.shape[1]
    total = before[...]
    step = min(TERM_STEP, ins.shape[1])
    for start in range(0, ins.shape[1], step):
        span = slice(start, start + step)
        places = lax.broadcasted_iota(jnp.int32, (inserts, step), 0)

        def values(left, right):
            chosen = (places == ins[right : right + 1, span]).astype(jnp.bfloat16)
            chosen = jnp.concatenate([chosen] * 3, axis=0)
            picked = jnp.dot(table, chosen, preferred_element_type=jnp.float32)
            here = places == ins[left : left + 1, span]
            return [
                jnp.sum(
                    jnp.where(here, picked[part * inserts : (part + 1) * inserts], 0.0),
                    axis=0,
                    keepdims=True,
                )
                for part in range(2 * pairs)
            ]

        first, second = values(0, 1), values(2, 3)
        scale = coef[:, span]
        sums = [jnp.zeros((1, step), jnp.float32) for _ in range(8)]
        for pair in range(pairs):
            a, b = first[2 * pair], first[2 * pair + 1]
            c, d = second[2 * pair], second[2 * pair + 1]
            real, imag = scale * (a * c - b * d), scale * (a * d + b * c)
            for apart in range(3):
                sums[2 * apart] += weight[3 * pair + apart] * real
                sums[2 * apart + 1] += weight[3 * pair + apart] * imag
        rows = thirds(jnp.concatenate(sums, axis=0), 0)
        bins = lax.broadcasted_iota(jnp.int32, (entries, step), 0)
        bins = (bins == entry[:, span]).astype(jnp.bfloat16)
        spread = nt_dot(rows, bins)
        total += spread[:8] + spread[8:16] + spread[16:]
    out[...] = total


def direct(tables, pairs, swap, weight, ins, coef, entry, before):
    size = tables[0].shape[0] // (2 if pairs == 3 else 1)
    smem = pl.BlockSpec(memory_space=pltpu.SMEM)
    vmem = pl.BlockSpec(memory_space=pltpu.VMEM)
    return pl.pallas_call(
        direct_kernel,
        in_specs=[smem, smem] + [vmem] * (4 + len(tables)),
        out_specs=vmem,
        out_shape=jax.ShapeDtypeStruct(before.shape, jnp.float32),
        scratch_shapes=[pltpu.VMEM((pairs * size, size // 2), jnp.float32)],
        cost_estimate=pl.CostEstimate(
            flops=2 * pairs * size * size * ins.shape[1] * 3,
            bytes_accessed=40 * ins.shape[1],
            transcendentals=0,
        ),
        name="direct",
    )(swap, weight, ins, coef, entry, before, *tables)


def after(value, *others):
    return lax.optimization_barrier((value,) + others)[0]


def total_over(value, axis):
    devices = lax.axis_size(axis)
    if devices & (devices - 1):
        return lax.psum(value, axis)
    distance = 1
    while distance < devices:
        value = value + lax.ppermute(value, axis, [(i, i ^ distance) for i in range(devices)])
        distance *= 2
    return value


def local(
    meson_fields, perambulators, direct_ins, direct_coef, direct_entry, box_ins, box_coef, box_entry
):
    devices = lax.axis_size("tm")
    owned = 4
    entries = owned * devices
    here = lax.axis_index("tm")
    role = here % GROUP
    everyone = range(devices)

    def move(value, target):
        route = [(i, target[i % GROUP](i) % devices) for i in everyone if i % GROUP in target]
        return lax.ppermute(value, "tm", route)

    def by_role(*choices):
        picked = jnp.asarray(choices[3])
        for number in range(3):
            picked = jnp.where(role == number, choices[number], picked)
        return picked

    fields = meson_fields[:, :, 0]
    factor = perambulators[:, 0]
    own = dress(fields, factor, 0, PARTS[:1])
    own = own + dress(fields, after(factor, own[0]), PARTS[0], PARTS[1:])
    count = len(own)
    half = count // 2

    across = {0: lambda i: i + 1, 1: lambda i: i + 2, 2: lambda i: i - 2, 3: lambda i: i - 1}
    along = {0: lambda i: i - GROUP, 3: lambda i: i + GROUP}
    beside = {0: lambda i: i + 1, 3: lambda i: i - 1}
    cross = {0: lambda i: i + 2, 3: lambda i: i - 2}

    terms = box_ins.shape[0]
    ins_table = box_ins.T
    swapped_table = ins_table[jnp.array([1, 0, 3, 2])]
    part = terms // 2
    late_table = jnp.where(role == 1, ins_table[:, part:], swapped_table[:, :part])
    send_table = jnp.where(role == 0, swapped_table[:, :part], ins_table[:, part:])
    late_entry = jnp.where(role == 1, box_entry[part:], box_entry[:part])
    late_coef = jnp.where(role == 1, box_coef[part:], box_coef[:part])

    near, far = [], []
    for chunk in range(count):
        near.append(move(own[chunk], across))
        far.append(move(own[chunk], along))
    rows = own[0].shape[2]
    cuts = [(j, 0, rows) for j in range(half - 1)]
    cuts += [(half - 1, 0, rows // 2), (half - 1, rows // 2, rows // 2)]
    split = [
        jnp.where(
            role == 0,
            own[half + j][:, :, start : start + length],
            own[j][:, :, start : start + length],
        )
        for j, start, length in cuts
    ]
    upper = jnp.where(role == 0, 0, 1).astype(jnp.int32)[None]
    shares = [slice(0, part // 2), slice(part // 2, part)]
    chosen = [send_table[row, share] for share in shares for row in (0, 2)]
    extra = pick(own, jnp.concatenate(chosen), upper, len(shares))
    mate = move(after(own[-1], extra[0]), beside)

    edge = (role == 0) | (role == 3)
    one, zero = jnp.float32(1.0), jnp.float32(0.0)

    def weights(first, second, third):
        return jnp.stack([first + zero, second + zero, third + zero])

    def box_table(table, entry, coef, weight, swap):
        scale = [weight[apart] * coef for apart in range(3)]
        scale.append(jnp.where(swap == 1, -one, one) * jnp.ones_like(coef))
        return jnp.concatenate([table, entry[None]]), jnp.stack(scale)

    def role_table(swap):
        return jnp.where(swap == 1, swapped_table, ins_table)

    def join(first, second):
        return tuple(jnp.concatenate([a, b], axis=1) for a, b in zip(first, second))

    outer = jnp.where(edge, one, zero)
    inner = one - outer
    same_weight = weights(one, zero, zero)
    near_weight = weights(zero, inner, outer)
    third_weight = weights(zero, by_role(zero, zero, one, zero), outer)
    split_weight = weights(zero, by_role(zero, one, zero, zero), zero)
    both_inner = weights(zero, inner, zero)
    near_swap = by_role(0, 1, 0, 1)
    third_swap = by_role(0, 0, 1, 1)
    size = 2 * fields.shape[1]
    with_entry = functools.partial(box_table, entry=box_entry, coef=box_coef)
    same_table = with_entry(ins_table, weight=same_weight, swap=0)
    near_table = with_entry(role_table(near_swap), weight=near_weight, swap=near_swap)
    third_table = with_entry(role_table(third_swap), weight=third_weight, swap=third_swap)
    both_table = join(near_table, third_table)
    late_swap = by_role(0, 0, 1, 0)
    late_tables = [
        box_table(late_table[:, share], late_entry[share], late_coef[share], both_inner, late_swap)
        for share in shares
    ]
    main_scalars = (
        jnp.stack([jnp.int32(0), near_swap, third_swap, edge.astype(jnp.int32)]),
        jnp.concatenate([same_weight, near_weight, third_weight]),
    )
    split_scalars = (jnp.zeros((4,), jnp.int32), split_weight)
    direct_terms = (direct_ins.T, direct_coef[None], direct_entry[None])
    small = (
        near_table, third_table, both_table, late_tables, main_scalars, split_scalars, direct_terms
    )

    total = box([(own, own, [])], same_table, jnp.zeros((8, entries), jnp.float32))
    table = jnp.zeros((2 * size, 3 * size), jnp.float32)
    (total, small, extra, split), _ = lax.optimization_barrier(((total, small, extra, split), near[0]))
    near_table, third_table, both_table, late_tables, main_scalars, split_scalars, direct_terms = small
    split_in, extra_in = [], []
    for piece in split:
        split_in.append(move(after(piece, near[-2]), cross))
    for piece in extra:
        extra_in.append(move(after(piece, near[-2]), cross))
    early = (total,)
    near_beside, far_beside = [], []
    for chunk in range(count):
        if chunk < count - 1:
            far_beside.append(move(after(far[chunk], *early), beside))
        near_beside.append(move(after(near[chunk], *early), beside))
        table = lax.cond(
            edge,
            lambda o, a, z, c, t: gram([o, a, z], 2, 3, t),
            lambda o, a, z, c, t: gram([o, a, c], 2, 3, t),
            own[chunk], near[chunk], far[chunk], near_beside[chunk], table,
        )
        early = (table,)
        if chunk == count - 2:
            total = lax.cond(
                edge,
                lambda o, m, k, t: t,
                lambda o, m, k, t: box([(o, m, [])], k, t),
                own, near[:-1] + [mate], near_table, after(total, table),
            )
            early = (table, total)
    far_beside.append(move(after(far[-1], table), beside))
    total = lax.cond(
        edge,
        lambda o, a, z, c, k, j, t: box([(o, a, []), (a, z, [])], j, t),
        lambda o, a, z, c, k, j, t: box([(o, c, [])], k, t),
        own, near, far, near_beside, third_table, both_table, after(total, table),
    )
    total = direct([table], 3, *main_scalars, *direct_terms, total)
    split_gram = after(jnp.zeros((size, size), jnp.float32), total)
    for piece, (j, start, _) in zip(split_in, cuts):
        split_gram = lax.cond(
            role == 1,
            lambda v, lo, hi, t, start=start: gram([v, lo], 1, 1, t, start),
            lambda v, lo, hi, t, start=start: gram([v, hi], 1, 1, t, start),
            piece, far_beside[j], far_beside[half + j], split_gram,
        )
    split_other = move(split_gram, {2: lambda i: i - 5})
    total = after(total, split_gram)
    for number in range(len(shares)):
        total = lax.cond(
            role == 1,
            lambda v, x, f, k, t: box([(v, f, [x])], k, t),
            lambda v, x, f, k, t: box([(v, f[half:] + f[:half], [x])], k, t),
            split_in, extra_in[number], far_beside, late_tables[number], total,
        )
        if number == 0:
            total = direct([split_gram, split_other], 1, *split_scalars, *direct_terms, total)
    summed = total_over(total, "tm") / devices
    mine = lax.dynamic_slice_in_dim(summed[:6], here * owned, owned, axis=1)
    return mine.reshape(3, 2, owned)


def solution(mesh):
    placed = (
        P(None, None, ("cfg", "tm"), None, None),
        P(None, ("cfg", "tm"), None, None),
        P(),
        P(),
        P(),
        P(),
        P(),
        P(),
    )

    return jax.shard_map(
        local, mesh=mesh, in_specs=placed, out_specs=P(None, None, ("cfg", "tm")), check_vma=False
    )
```

```python
import functools

import jax
import jax.numpy as jnp
from jax import lax
from jax.experimental import pallas as pl
from jax.experimental.pallas import tpu as pltpu
from jax.sharding import PartitionSpec as P

PARTS = (1, 1, 1, 1)
GROUP = 4
STEP_ROWS = 16
STEP_INS = 8
TERM_STEP = 512
NT = (((1,), (1,)), ((), ()))


def nt_dot(left, right):
    return lax.dot_general(left, right, NT, preferred_element_type=jnp.float32)


def dress_kernel(out_steps, fields, factor, *refs):
    outs, weight = refs[:-1], refs[-1]
    modes = factor.shape[-1]
    step = pl.program_id(0)

    @pl.when(step == 0)
    def _():
        weight[:modes, :modes] = factor[0]
        weight[:modes, modes:] = factor[1]
        weight[modes:, :modes] = -factor[1]
        weight[modes:, modes:] = factor[0]

    inserts, rows = fields.shape[1:3]
    sides = fields[...].reshape(2, inserts * rows, modes)
    product = jnp.dot(
        jnp.concatenate([sides[0], sides[1]], axis=1),
        weight[...],
        preferred_element_type=jnp.float32,
    )
    first = 0
    for out, count in zip(outs, out_steps):

        @pl.when((step >= first) & (step < first + count))
        def _(out=out):
            out[0] = product[:, :modes].reshape(inserts, rows, modes).astype(out.dtype)
            out[1] = product[:, modes:].reshape(inserts, rows, modes).astype(out.dtype)

        first += count


def dress(fields, factor, first, parts):
    inserts, modes = fields.shape[1], fields.shape[-1]
    rows = modes // sum(PARTS)
    steps = inserts // STEP_INS
    block = (2, STEP_INS, rows, modes)
    total = sum(parts)

    def place(before, part):
        def where(g):
            own = jnp.clip(g - before * steps, 0, part * steps - 1)
            return 0, own % steps, own // steps, 0

        return where

    return pl.pallas_call(
        functools.partial(dress_kernel, [part * steps for part in parts]),
        grid=(total * steps,),
        in_specs=[
            pl.BlockSpec(block, lambda g: (0, g % steps, first + g // steps, 0)),
            pl.BlockSpec((2, modes, modes), lambda g: (0, 0, 0)),
        ],
        out_specs=[
            pl.BlockSpec(block, place(sum(parts[:number]), part))
            for number, part in enumerate(parts)
        ],
        out_shape=[
            jax.ShapeDtypeStruct((2, inserts, part * rows, modes), fields.dtype) for part in parts
        ],
        scratch_shapes=[pltpu.VMEM((2 * modes, 2 * modes), fields.dtype)],
        cost_estimate=pl.CostEstimate(
            flops=16 * total * inserts * rows * modes * modes,
            bytes_accessed=8 * total * inserts * rows * modes,
            transcendentals=0,
        ),
        name="dress",
    )(fields, factor)


def gram_kernel(count, left_count, *refs):
    blocks, before, out, flat = refs[:count], refs[count], refs[count + 1], refs[count + 2]
    _, inserts, rows, modes = blocks[0].shape
    size = 2 * inserts
    for index, block in enumerate(blocks):
        flat[index * size : (index + 1) * size] = block[...].reshape(size, rows * modes)
    product = nt_dot(flat[: left_count * size], flat[(count - out.shape[1] // size) * size :])

    @pl.when(pl.program_id(0) == 0)
    def _():
        out[...] = before[...] + product

    @pl.when(pl.program_id(0) > 0)
    def _():
        out[...] += product


def gram(blocks, left_count, right_count, before, offset=0):
    count = len(blocks)
    _, inserts, rows, modes = blocks[0].shape
    size = 2 * inserts
    block = (2, inserts, STEP_ROWS, modes)
    spec = pl.BlockSpec(block, lambda i: (0, 0, i, 0))
    last = pl.BlockSpec(block, lambda i: (0, 0, offset // STEP_ROWS + i, 0))
    shape = (left_count * size, right_count * size)
    whole = pl.BlockSpec(shape, lambda i: (0, 0))
    return pl.pallas_call(
        functools.partial(gram_kernel, count, left_count),
        grid=(rows // STEP_ROWS,),
        in_specs=[spec] * (count - 1) + [last, whole],
        out_specs=whole,
        out_shape=jax.ShapeDtypeStruct(shape, jnp.float32),
        scratch_shapes=[pltpu.VMEM((count * size, STEP_ROWS * modes), jnp.bfloat16)],
        cost_estimate=pl.CostEstimate(
            flops=16 * shape[0] * shape[1] * rows * modes,
            bytes_accessed=count * 2 * size * rows * modes,
            transcendentals=0,
        ),
        name="gram",
    )(*blocks, before)


def box_kernel(counts, turned, ins, scale, *refs):
    groups = []
    for left_count, right_count, extra_count in counts:
        left, refs = refs[:left_count], refs[left_count:]
        right, refs = refs[:right_count], refs[right_count:]
        extra, refs = refs[:extra_count], refs[extra_count:]
        groups.append((left, right, extra))
    out, held, sems = refs
    terms = held.shape[0] // len(groups)

    def fetch(group, term):
        left, right, extra = groups[group]
        slot = group * terms + term
        for place in range(4):
            where = ins[place, slot]
            sources = [ref.at[:, where] for ref in (right if place % 2 else left)]
            if place % 2 == 0:
                for ref in extra:
                    where = (place // 2) * terms + term
                    sources += [ref.at[number, :, where] for number in range(ref.shape[0])]
            start = 0
            for source in sources:
                rows = source.shape[1]
                target = start
                if place % 2 == 1 and turned:
                    target = lax.rem(start + ins[5, slot], held.shape[3])
                    target = pl.multiple_of(target, rows)
                pltpu.make_async_copy(
                    source, held.at[slot, place, :, pl.ds(target, rows)], sems.at[slot]
                ).start()
                start += rows

    @pl.loop(0, terms)
    def _(term):
        fetch(0, term)

    def product(slot, one, other):
        real, imag = held[slot, one, 0], held[slot, one, 1]
        other_side = jnp.concatenate([held[slot, other, 0], held[slot, other, 1]], axis=1)
        return (
            nt_dot(jnp.concatenate([real, imag], axis=1), other_side),
            nt_dot(jnp.concatenate([imag, -real], axis=1), other_side),
        )

    out[...] = jnp.zeros_like(out)
    spot = lax.broadcasted_iota(jnp.int32, out.shape, 1)
    line = lax.broadcasted_iota(jnp.int32, out.shape, 0)
    for group in range(len(groups)):

        @pl.loop(0, terms)
        def _(term, group=group):
            if group + 1 < len(groups):
                fetch(group + 1, term)
            slot = group * terms + term
            pltpu.make_async_copy(held.at[slot], held.at[slot], sems.at[slot]).wait()
            first_real, first_imag = product(slot, 0, 1)
            second_real, second_imag = product(slot, 3, 2)
            real = jnp.sum(first_real * second_real + first_imag * second_imag)
            imag = jnp.sum(first_imag * second_real - first_real * second_imag)
            imag = imag * scale[3, slot]
            added = jnp.zeros(out.shape, jnp.float32)
            for apart in range(3):
                added = jnp.where(line == 2 * apart, real * scale[apart, slot], added)
                added = jnp.where(line == 2 * apart + 1, imag * scale[apart, slot], added)
            out[...] -= jnp.where(spot == ins[4, slot], added, 0.0)


def box(groups, table, entries, turned=False):
    ins, scale = table
    slots = ins.shape[1]
    modes = groups[0][0][0].shape[3]
    kind = groups[0][0][0].dtype
    arrays = [ref for group in groups for refs in group for ref in refs]
    smem = pl.BlockSpec(memory_space=pltpu.SMEM)
    vmem = pl.BlockSpec(memory_space=pltpu.VMEM)
    return pl.pallas_call(
        functools.partial(
            box_kernel, [tuple(len(refs) for refs in group) for group in groups], turned
        ),
        in_specs=[smem, smem] + [pl.BlockSpec(memory_space=pl.ANY)] * len(arrays),
        out_specs=vmem,
        out_shape=jax.ShapeDtypeStruct((8, entries), jnp.float32),
        scratch_shapes=[
            pltpu.VMEM((slots, 4, 2, modes, modes), kind),
            pltpu.SemaphoreType.DMA((slots,)),
        ],
        cost_estimate=pl.CostEstimate(
            flops=32 * slots * modes * modes * modes,
            bytes_accessed=16 * slots * modes * modes,
            transcendentals=0,
        ),
        name="box",
    )(ins, scale, *arrays)


def pick_kernel(count, upper, places, *refs):
    blocks, outs, (held, sems) = refs[:count], refs[count:-2], refs[-2:]
    terms = places.shape[0]

    def fetch(term):
        def go(sources, start=0):
            for source in sources:
                pltpu.make_async_copy(
                    source, held.at[term, :, pl.ds(start, source.shape[1])], sems.at[term]
                ).start()
                start += source.shape[1]

        where = places[term]

        @pl.when(upper[0] == 1)
        def _():
            go([ref.at[:, where] for ref in blocks[count // 2 :]])

        @pl.when(upper[0] == 0)
        def _():
            go([ref.at[:, where] for ref in blocks[: count // 2]])

    for term in range(terms):
        fetch(term)
    share = terms // len(outs)
    for term in range(terms):
        pltpu.make_async_copy(held.at[term], held.at[term], sems.at[term]).wait()
        target = outs[term // share].at[0, :, term % share]
        pltpu.make_async_copy(held.at[term], target, sems.at[term]).start()
    for term in range(terms):
        target = outs[term // share].at[0, :, term % share]
        pltpu.make_async_copy(held.at[term], target, sems.at[term]).wait()


def pick(blocks, places, upper, shares):
    modes = blocks[0].shape[3]
    rows = modes // 2
    count = places.shape[0]
    smem = pl.BlockSpec(memory_space=pltpu.SMEM)
    hbm = pl.BlockSpec(memory_space=pl.ANY)
    return pl.pallas_call(
        functools.partial(pick_kernel, len(blocks)),
        in_specs=[smem, smem] + [hbm] * len(blocks),
        out_specs=[hbm] * shares,
        out_shape=[
            jax.ShapeDtypeStruct((1, 2, count // shares, rows, modes), blocks[0].dtype)
        ] * shares,
        scratch_shapes=[
            pltpu.VMEM((count, 2, rows, modes), blocks[0].dtype),
            pltpu.SemaphoreType.DMA((count,)),
        ],
        cost_estimate=pl.CostEstimate(
            flops=0, bytes_accessed=8 * count * rows * modes, transcendentals=0
        ),
        name="pick",
    )(upper, places, *blocks)


def thirds(value, axis):
    high = value.astype(jnp.bfloat16)
    rest = value - high.astype(jnp.float32)
    middle = rest.astype(jnp.bfloat16)
    low = (rest - middle.astype(jnp.float32)).astype(jnp.bfloat16)
    return jnp.concatenate([high, middle, low], axis=axis)


def direct_kernel(swap, weight, ins, coef, entry, *refs):
    tables, out, lines = refs[:-2], refs[-2], refs[-1]
    size = 2 * lines.shape[1]
    inserts = size // 2
    if len(tables) == 1:
        grams = [tables[0][:size, place * size : (place + 1) * size] for place in range(3)]
        below = tables[0][size:, 2 * size :]
        grams[2] = jnp.where(swap[3] == 1, below, grams[2])
    else:
        grams = [tables[0][...] + tables[1][...].T]
    pairs = len(grams)
    for pair, table in enumerate(grams):
        table = jnp.where(swap[pair] == 1, table.T, table)
        upper, lower = table[:inserts], table[inserts:]
        lines[pair * size : pair * size + inserts] = upper[:, :inserts] + lower[:, inserts:]
        lines[pair * size + inserts : (pair + 1) * size] = lower[:, :inserts] - upper[:, inserts:]
    table = thirds(lines[...], 1)
    entries = out.shape[1]
    total = jnp.zeros(out.shape, jnp.float32)
    step = min(TERM_STEP, ins.shape[1])
    for start in range(0, ins.shape[1], step):
        span = slice(start, start + step)
        places = lax.broadcasted_iota(jnp.int32, (inserts, step), 0)

        def values(left, right):
            chosen = (places == ins[right : right + 1, span]).astype(jnp.bfloat16)
            chosen = jnp.concatenate([chosen] * 3, axis=0)
            picked = jnp.dot(table, chosen, preferred_element_type=jnp.float32)
            here = places == ins[left : left + 1, span]
            return [
                jnp.sum(
                    jnp.where(here, picked[part * inserts : (part + 1) * inserts], 0.0),
                    axis=0,
                    keepdims=True,
                )
                for part in range(2 * pairs)
            ]

        first, second = values(0, 1), values(2, 3)
        scale = coef[:, span]
        sums = [jnp.zeros((1, step), jnp.float32) for _ in range(8)]
        for pair in range(pairs):
            a, b = first[2 * pair], first[2 * pair + 1]
            c, d = second[2 * pair], second[2 * pair + 1]
            real, imag = scale * (a * c - b * d), scale * (a * d + b * c)
            for apart in range(3):
                sums[2 * apart] += weight[3 * pair + apart] * real
                sums[2 * apart + 1] += weight[3 * pair + apart] * imag
        rows = thirds(jnp.concatenate(sums, axis=0), 0)
        bins = lax.broadcasted_iota(jnp.int32, (entries, step), 0)
        bins = (bins == entry[:, span]).astype(jnp.bfloat16)
        spread = nt_dot(rows, bins)
        total += spread[:8] + spread[8:16] + spread[16:]
    out[...] = total


def direct(tables, pairs, swap, weight, ins, coef, entry, entries):
    size = tables[0].shape[0] // (2 if pairs == 3 else 1)
    smem = pl.BlockSpec(memory_space=pltpu.SMEM)
    vmem = pl.BlockSpec(memory_space=pltpu.VMEM)
    return pl.pallas_call(
        direct_kernel,
        in_specs=[smem, smem] + [vmem] * (3 + len(tables)),
        out_specs=vmem,
        out_shape=jax.ShapeDtypeStruct((8, entries), jnp.float32),
        scratch_shapes=[pltpu.VMEM((pairs * size, size // 2), jnp.float32)],
        cost_estimate=pl.CostEstimate(
            flops=2 * pairs * size * size * ins.shape[1] * 3,
            bytes_accessed=40 * ins.shape[1],
            transcendentals=0,
        ),
        name="direct",
    )(swap, weight, ins, coef, entry, *tables)


def after(value, *others):
    return lax.optimization_barrier((value,) + others)[0]


def total_over(value, axis):
    devices = lax.axis_size(axis)
    if devices & (devices - 1):
        return lax.psum(value, axis)
    distance = 1
    while distance < devices:
        value = value + lax.ppermute(value, axis, [(i, i ^ distance) for i in range(devices)])
        distance *= 2
    return value


def local(
    meson_fields, perambulators, direct_ins, direct_coef, direct_entry, box_ins, box_coef, box_entry
):
    devices = lax.axis_size("tm")
    owned = 4
    entries = owned * devices
    here = lax.axis_index("tm")
    role = here % GROUP
    everyone = range(devices)

    def move(value, target):
        route = [(i, target[i % GROUP](i) % devices) for i in everyone if i % GROUP in target]
        return lax.ppermute(value, "tm", route)

    def by_role(*choices):
        picked = jnp.asarray(choices[3])
        for number in range(3):
            picked = jnp.where(role == number, choices[number], picked)
        return picked

    fields = meson_fields[:, :, 0]
    factor = perambulators[:, 0]
    own = dress(fields, factor, 0, PARTS[:1])
    own = own + dress(fields, after(factor, own[0]), PARTS[0], PARTS[1:])
    count = len(own)
    half = count // 2

    across = {0: lambda i: i + 1, 1: lambda i: i + 2, 2: lambda i: i - 2, 3: lambda i: i - 1}
    along = {0: lambda i: i - GROUP, 3: lambda i: i + GROUP}
    beside = {0: lambda i: i + 1, 3: lambda i: i - 1}
    cross = {0: lambda i: i + 2, 3: lambda i: i - 2}

    terms = box_ins.shape[0]
    ins_table = box_ins.T
    swapped_table = ins_table[jnp.array([1, 0, 3, 2])]
    part = terms // 2
    late_table = jnp.where(role == 1, ins_table[:, part:], swapped_table[:, :part])
    send_table = jnp.where(role == 0, swapped_table[:, :part], ins_table[:, part:])
    late_entry = jnp.where(role == 1, box_entry[part:], box_entry[:part])
    late_coef = jnp.where(role == 1, box_coef[part:], box_coef[:part])

    near, far = [], []
    for chunk in range(count):
        near.append(move(own[chunk], across))
        far.append(move(own[chunk], along))
    rows = own[0].shape[2]
    cuts = [(j, 0, rows) for j in range(half - 1)]
    cuts += [(half - 1, 0, rows // 2), (half - 1, rows // 2, rows // 2)]
    split = [
        jnp.where(
            role == 0,
            own[half + j][:, :, start : start + length],
            own[j][:, :, start : start + length],
        )
        for j, start, length in cuts
    ]
    upper = jnp.where(role == 0, 0, 1).astype(jnp.int32)[None]
    shares = [slice(0, part // 2), slice(part // 2, part)]
    chosen = [send_table[row, share] for share in shares for row in (0, 2)]
    extra = pick(own, jnp.concatenate(chosen), upper, len(shares))
    mate = move(after(own[-1], extra[0]), beside)

    edge = (role == 0) | (role == 3)
    one, zero = jnp.float32(1.0), jnp.float32(0.0)

    def weights(first, second, third):
        return jnp.stack([first + zero, second + zero, third + zero])

    def box_table(table, entry, coef, weight, swap):
        scale = [weight[apart] * coef for apart in range(3)]
        scale.append(jnp.where(swap == 1, -one, one) * jnp.ones_like(coef))
        return jnp.concatenate([table, entry[None]]), jnp.stack(scale)

    def role_table(swap):
        return jnp.where(swap == 1, swapped_table, ins_table)

    def join(first, second):
        return tuple(jnp.concatenate([a, b], axis=1) for a, b in zip(first, second))

    outer = jnp.where(edge, one, zero)
    inner = one - outer
    same_weight = weights(one, zero, zero)
    near_weight = weights(zero, inner, outer)
    third_weight = weights(zero, by_role(zero, zero, one, zero), outer)
    split_weight = weights(zero, by_role(zero, one, zero, zero), zero)
    both_inner = weights(zero, inner, zero)
    near_swap = by_role(0, 1, 0, 1)
    third_swap = by_role(0, 0, 1, 1)
    size = 2 * fields.shape[1]
    with_entry = functools.partial(box_table, entry=box_entry, coef=box_coef)
    same_table = with_entry(ins_table, weight=same_weight, swap=0)
    near_table = with_entry(role_table(near_swap), weight=near_weight, swap=near_swap)
    third_table = with_entry(role_table(third_swap), weight=third_weight, swap=third_swap)
    both_table = join(near_table, third_table)
    late_swap = by_role(0, 0, 1, 0)
    late_ins, late_scale = box_table(late_table, late_entry, late_coef, both_inner, late_swap)
    turn = by_role(0, 0, fields.shape[2] // 2, 0) + jnp.zeros_like(late_entry)
    late_ins = jnp.concatenate([late_ins, turn[None]])
    late_tables = [(late_ins[:, share], late_scale[:, share]) for share in shares]
    main_scalars = (
        jnp.stack([jnp.int32(0), near_swap, third_swap, edge.astype(jnp.int32)]),
        jnp.concatenate([same_weight, near_weight, third_weight]),
    )
    split_scalars = (main_scalars[0], split_weight)
    direct_terms = (direct_ins.T, direct_coef[None], direct_entry[None])
    small = (
        near_table, third_table, both_table, late_tables, main_scalars, split_scalars, direct_terms
    )

    total = box([(own, own, [])], same_table, entries)
    table = jnp.zeros((2 * size, 3 * size), jnp.float32)
    (total, small, extra, split), _ = lax.optimization_barrier(((total, small, extra, split), near[0]))
    near_table, third_table, both_table, late_tables, main_scalars, split_scalars, direct_terms = small
    split_in, extra_in = [], []
    for piece in split:
        split_in.append(move(after(piece, near[-2]), cross))
    for piece in extra:
        extra_in.append(move(after(piece, near[-2]), cross))
    early = (total,)
    near_beside, far_beside = [], []
    for chunk in range(count):
        if chunk < count - 1:
            far_beside.append(move(after(far[chunk], *early), beside))
        near_beside.append(move(after(near[chunk], *early), beside))
        table = lax.cond(
            edge,
            lambda o, a, z, c, t: gram([o, a, z], 2, 3, t),
            lambda o, a, z, c, t: gram([o, a, c], 2, 3, t),
            own[chunk], near[chunk], far[chunk], near_beside[chunk], table,
        )
        early = (table,)
        if chunk == count - 2:
            total += lax.cond(
                edge,
                lambda o, m, k: jnp.zeros((8, entries), jnp.float32),
                lambda o, m, k: box([(o, m, [])], k, entries),
                own, near[:-1] + [mate], after(near_table, table),
            )
            early = (table, total)
    far_beside.append(move(after(far[-1], table), beside))
    third_table, both_table = after((third_table, both_table), table)
    third = lax.cond(
        edge,
        lambda o, a, z, c, k, j: box([(o, a, []), (a, z, [])], j, entries),
        lambda o, a, z, c, k, j: box([(o, c, [])], k, entries),
        own, near, far, near_beside, third_table, both_table,
    )
    main = direct([table], 3, *after(main_scalars, third), *direct_terms, entries)
    branch = by_role(0, 1, 2, 0)
    split_gram = after(jnp.zeros((size, size), jnp.float32), main)
    for piece, (j, start, _) in zip(split_in, cuts):
        split_gram = lax.switch(
            branch,
            [
                lambda v, lo, hi, t: jnp.zeros_like(t),
                lambda v, lo, hi, t, start=start: gram([v, lo], 1, 1, t, start),
                lambda v, lo, hi, t, start=start: gram([v, hi], 1, 1, t, start),
            ],
            piece, far_beside[j], far_beside[half + j], split_gram,
        )
    split_other = move(split_gram, {2: lambda i: i - 5})
    total += third + main
    token = split_gram
    late = []
    for number in range(len(shares)):
        token = lax.cond(
            edge,
            lambda v, f, x, k: jnp.zeros((8, entries), jnp.float32),
            lambda v, f, x, k: box([(v, f, [x])], k, entries, turned=True),
            split_in, far_beside, extra_in[number], after(late_tables[number], token),
        )
        late.append(token)
        if number == 0:
            scalars = after(split_scalars, token)
            token = lax.cond(
                role == 1,
                lambda a, b, k, d: direct([a, b], 1, *k, *d, entries),
                lambda a, b, k, d: jnp.zeros((8, entries), jnp.float32),
                split_gram, split_other, scalars, direct_terms,
            )
            late.append(token)
    total += sum(late)
    summed = total_over(total, "tm") / devices
    mine = lax.dynamic_slice_in_dim(summed[:6], here * owned, owned, axis=1)
    return mine.reshape(3, 2, owned)


def solution(mesh):
    placed = (
        P(None, None, ("cfg", "tm"), None, None),
        P(None, ("cfg", "tm"), None, None),
        P(),
        P(),
        P(),
        P(),
        P(),
        P(),
    )

    return jax.shard_map(
        local, mesh=mesh, in_specs=placed, out_specs=P(None, None, ("cfg", "tm")), check_vma=False
    )
```

```python
import functools

import jax
import jax.numpy as jnp
from jax import lax
from jax.experimental import pallas as pl
from jax.experimental.pallas import tpu as pltpu
from jax.sharding import PartitionSpec as P

PARTS = (1, 1, 1, 1)
GROUP = 4
STEP_ROWS = 32
STEP_INS = 16
TERM_STEP = 1024
NT = (((1,), (1,)), ((), ()))


def nt_dot(left, right):
    return lax.dot_general(left, right, NT, preferred_element_type=jnp.float32)


def dress_kernel(out_steps, fields, factor, *refs):
    outs, weight = refs[:-1], refs[-1]
    modes = factor.shape[-1]
    step = pl.program_id(0)

    @pl.when(step == 0)
    def _():
        weight[:modes, :modes] = factor[0]
        weight[:modes, modes:] = factor[1]
        weight[modes:, :modes] = -factor[1]
        weight[modes:, modes:] = factor[0]

    inserts, rows = fields.shape[1:3]
    sides = fields[...].reshape(2, inserts * rows, modes)
    product = jnp.dot(
        jnp.concatenate([sides[0], sides[1]], axis=1),
        weight[...],
        preferred_element_type=jnp.float32,
    )
    first = 0
    for out, count in zip(outs, out_steps):

        @pl.when((step >= first) & (step < first + count))
        def _(out=out):
            out[0] = product[:, :modes].reshape(inserts, rows, modes).astype(out.dtype)
            out[1] = product[:, modes:].reshape(inserts, rows, modes).astype(out.dtype)

        first += count


def dress(fields, factor, first, parts):
    inserts, modes = fields.shape[1], fields.shape[-1]
    rows = modes // sum(PARTS)
    steps = inserts // STEP_INS
    block = (2, STEP_INS, rows, modes)
    total = sum(parts)

    def place(before, part):
        def where(g):
            own = jnp.clip(g - before * steps, 0, part * steps - 1)
            return 0, own % steps, own // steps, 0

        return where

    return pl.pallas_call(
        functools.partial(dress_kernel, [part * steps for part in parts]),
        grid=(total * steps,),
        in_specs=[
            pl.BlockSpec(block, lambda g: (0, g % steps, first + g // steps, 0)),
            pl.BlockSpec((2, modes, modes), lambda g: (0, 0, 0)),
        ],
        out_specs=[
            pl.BlockSpec(block, place(sum(parts[:number]), part))
            for number, part in enumerate(parts)
        ],
        out_shape=[
            jax.ShapeDtypeStruct((2, inserts, part * rows, modes), fields.dtype) for part in parts
        ],
        scratch_shapes=[pltpu.VMEM((2 * modes, 2 * modes), fields.dtype)],
        cost_estimate=pl.CostEstimate(
            flops=16 * total * inserts * rows * modes * modes,
            bytes_accessed=8 * total * inserts * rows * modes,
            transcendentals=0,
        ),
        name="dress",
    )(fields, factor)


def gram_kernel(count, left_count, *refs):
    blocks, before, out, flat = refs[:count], refs[count], refs[count + 1], refs[count + 2]
    _, inserts, rows, modes = blocks[0].shape
    size = 2 * inserts
    for index, block in enumerate(blocks):
        flat[index * size : (index + 1) * size] = block[...].reshape(size, rows * modes)
    product = nt_dot(flat[: left_count * size], flat[(count - out.shape[1] // size) * size :])

    @pl.when(pl.program_id(0) == 0)
    def _():
        out[...] = before[...] + product

    @pl.when(pl.program_id(0) > 0)
    def _():
        out[...] += product


def gram(blocks, left_count, right_count, before, offset=0):
    count = len(blocks)
    _, inserts, rows, modes = blocks[0].shape
    size = 2 * inserts
    block = (2, inserts, STEP_ROWS, modes)
    spec = pl.BlockSpec(block, lambda i: (0, 0, i, 0))
    last = pl.BlockSpec(block, lambda i: (0, 0, offset // STEP_ROWS + i, 0))
    shape = (left_count * size, right_count * size)
    whole = pl.BlockSpec(shape, lambda i: (0, 0))
    return pl.pallas_call(
        functools.partial(gram_kernel, count, left_count),
        grid=(rows // STEP_ROWS,),
        in_specs=[spec] * (count - 1) + [last, whole],
        out_specs=whole,
        out_shape=jax.ShapeDtypeStruct(shape, jnp.float32),
        scratch_shapes=[pltpu.VMEM((count * size, STEP_ROWS * modes), jnp.bfloat16)],
        cost_estimate=pl.CostEstimate(
            flops=16 * shape[0] * shape[1] * rows * modes,
            bytes_accessed=count * 2 * size * rows * modes,
            transcendentals=0,
        ),
        name="gram",
    )(*blocks, before)


def box_kernel(counts, turned, ins, scale, *refs):
    groups = []
    for left_count, right_count, extra_count in counts:
        left, refs = refs[:left_count], refs[left_count:]
        right, refs = refs[:right_count], refs[right_count:]
        extra, refs = refs[:extra_count], refs[extra_count:]
        groups.append((left, right, extra))
    out, held, sems = refs
    terms = held.shape[0] // len(groups)

    def fetch(group, term):
        left, right, extra = groups[group]
        slot = group * terms + term
        for place in range(4):
            where = ins[place, slot]
            sources = [ref.at[:, where] for ref in (right if place % 2 else left)]
            if place % 2 == 0:
                for ref in extra:
                    where = (place // 2) * terms + term
                    sources += [ref.at[number, :, where] for number in range(ref.shape[0])]
            start = 0
            for source in sources:
                rows = source.shape[1]
                target = start
                if place % 2 == 1 and turned:
                    target = lax.rem(start + ins[5, slot], held.shape[3])
                    target = pl.multiple_of(target, rows)
                pltpu.make_async_copy(
                    source, held.at[slot, place, :, pl.ds(target, rows)], sems.at[slot]
                ).start()
                start += rows

    @pl.loop(0, terms)
    def _(term):
        fetch(0, term)

    def product(slot, one, other):
        real, imag = held[slot, one, 0], held[slot, one, 1]
        other_side = jnp.concatenate([held[slot, other, 0], held[slot, other, 1]], axis=1)
        return (
            nt_dot(jnp.concatenate([real, imag], axis=1), other_side),
            nt_dot(jnp.concatenate([imag, -real], axis=1), other_side),
        )

    out[...] = jnp.zeros_like(out)
    spot = lax.broadcasted_iota(jnp.int32, out.shape, 1)
    line = lax.broadcasted_iota(jnp.int32, out.shape, 0)
    for group in range(len(groups)):

        @pl.loop(0, terms)
        def _(term, group=group):
            if group + 1 < len(groups):
                fetch(group + 1, term)
            slot = group * terms + term
            pltpu.make_async_copy(held.at[slot], held.at[slot], sems.at[slot]).wait()
            first_real, first_imag = product(slot, 0, 1)
            second_real, second_imag = product(slot, 3, 2)
            real = jnp.sum(first_real * second_real + first_imag * second_imag)
            imag = jnp.sum(first_imag * second_real - first_real * second_imag)
            imag = imag * scale[3, slot]
            added = jnp.zeros(out.shape, jnp.float32)
            for apart in range(3):
                added = jnp.where(line == 2 * apart, real * scale[apart, slot], added)
                added = jnp.where(line == 2 * apart + 1, imag * scale[apart, slot], added)
            out[...] -= jnp.where(spot == ins[4, slot], added, 0.0)


def box(groups, table, entries, turned=False):
    ins, scale = table
    slots = ins.shape[1]
    modes = groups[0][0][0].shape[3]
    kind = groups[0][0][0].dtype
    arrays = [ref for group in groups for refs in group for ref in refs]
    smem = pl.BlockSpec(memory_space=pltpu.SMEM)
    vmem = pl.BlockSpec(memory_space=pltpu.VMEM)
    return pl.pallas_call(
        functools.partial(
            box_kernel, [tuple(len(refs) for refs in group) for group in groups], turned
        ),
        in_specs=[smem, smem] + [pl.BlockSpec(memory_space=pl.ANY)] * len(arrays),
        out_specs=vmem,
        out_shape=jax.ShapeDtypeStruct((8, entries), jnp.float32),
        scratch_shapes=[
            pltpu.VMEM((slots, 4, 2, modes, modes), kind),
            pltpu.SemaphoreType.DMA((slots,)),
        ],
        cost_estimate=pl.CostEstimate(
            flops=32 * slots * modes * modes * modes,
            bytes_accessed=16 * slots * modes * modes,
            transcendentals=0,
        ),
        name="box",
    )(ins, scale, *arrays)


def pick_kernel(count, upper, places, *refs):
    blocks, outs, (held, sems) = refs[:count], refs[count:-2], refs[-2:]
    terms = places.shape[0]

    def fetch(term):
        def go(sources, start=0):
            for source in sources:
                pltpu.make_async_copy(
                    source, held.at[term, :, pl.ds(start, source.shape[1])], sems.at[term]
                ).start()
                start += source.shape[1]

        where = places[term]

        @pl.when(upper[0] == 1)
        def _():
            go([ref.at[:, where] for ref in blocks[count // 2 :]])

        @pl.when(upper[0] == 0)
        def _():
            go([ref.at[:, where] for ref in blocks[: count // 2]])

    for term in range(terms):
        fetch(term)
    share = terms // len(outs)
    for term in range(terms):
        pltpu.make_async_copy(held.at[term], held.at[term], sems.at[term]).wait()
        target = outs[term // share].at[0, :, term % share]
        pltpu.make_async_copy(held.at[term], target, sems.at[term]).start()
    for term in range(terms):
        target = outs[term // share].at[0, :, term % share]
        pltpu.make_async_copy(held.at[term], target, sems.at[term]).wait()


def pick(blocks, places, upper, shares):
    modes = blocks[0].shape[3]
    rows = modes // 2
    count = places.shape[0]
    smem = pl.BlockSpec(memory_space=pltpu.SMEM)
    hbm = pl.BlockSpec(memory_space=pl.ANY)
    return pl.pallas_call(
        functools.partial(pick_kernel, len(blocks)),
        in_specs=[smem, smem] + [hbm] * len(blocks),
        out_specs=[hbm] * shares,
        out_shape=[
            jax.ShapeDtypeStruct((1, 2, count // shares, rows, modes), blocks[0].dtype)
        ] * shares,
        scratch_shapes=[
            pltpu.VMEM((count, 2, rows, modes), blocks[0].dtype),
            pltpu.SemaphoreType.DMA((count,)),
        ],
        cost_estimate=pl.CostEstimate(
            flops=0, bytes_accessed=8 * count * rows * modes, transcendentals=0
        ),
        name="pick",
    )(upper, places, *blocks)


def thirds(value, axis):
    high = value.astype(jnp.bfloat16)
    rest = value - high.astype(jnp.float32)
    middle = rest.astype(jnp.bfloat16)
    low = (rest - middle.astype(jnp.float32)).astype(jnp.bfloat16)
    return jnp.concatenate([high, middle, low], axis=axis)


def direct_kernel(swap, weight, ins, coef, entry, *refs):
    tables, out, lines = refs[:-2], refs[-2], refs[-1]
    size = 2 * lines.shape[1]
    inserts = size // 2
    if len(tables) == 1:
        grams = [tables[0][:size, place * size : (place + 1) * size] for place in range(3)]
        below = tables[0][size:, 2 * size :]
        grams[2] = jnp.where(swap[3] == 1, below, grams[2])
    else:
        grams = [tables[0][...] + tables[1][...].T]
    pairs = len(grams)
    for pair, table in enumerate(grams):
        table = jnp.where(swap[pair] == 1, table.T, table)
        upper, lower = table[:inserts], table[inserts:]
        lines[pair * size : pair * size + inserts] = upper[:, :inserts] + lower[:, inserts:]
        lines[pair * size + inserts : (pair + 1) * size] = lower[:, :inserts] - upper[:, inserts:]
    table = thirds(lines[...], 1)
    entries = out.shape[1]
    total = jnp.zeros(out.shape, jnp.float32)
    step = min(TERM_STEP, ins.shape[1])
    for start in range(0, ins.shape[1], step):
        span = slice(start, start + step)
        places = lax.broadcasted_iota(jnp.int32, (inserts, step), 0)

        def values(left, right):
            chosen = (places == ins[right : right + 1, span]).astype(jnp.bfloat16)
            chosen = jnp.concatenate([chosen] * 3, axis=0)
            picked = jnp.dot(table, chosen, preferred_element_type=jnp.float32)
            here = places == ins[left : left + 1, span]
            return [
                jnp.sum(
                    jnp.where(here, picked[part * inserts : (part + 1) * inserts], 0.0),
                    axis=0,
                    keepdims=True,
                )
                for part in range(2 * pairs)
            ]

        first, second = values(0, 1), values(2, 3)
        scale = coef[:, span]
        sums = [jnp.zeros((1, step), jnp.float32) for _ in range(8)]
        for pair in range(pairs):
            a, b = first[2 * pair], first[2 * pair + 1]
            c, d = second[2 * pair], second[2 * pair + 1]
            real, imag = scale * (a * c - b * d), scale * (a * d + b * c)
            for apart in range(3):
                sums[2 * apart] += weight[3 * pair + apart] * real
                sums[2 * apart + 1] += weight[3 * pair + apart] * imag
        rows = thirds(jnp.concatenate(sums, axis=0), 0)
        bins = lax.broadcasted_iota(jnp.int32, (entries, step), 0)
        bins = (bins == entry[:, span]).astype(jnp.bfloat16)
        spread = nt_dot(rows, bins)
        total += spread[:8] + spread[8:16] + spread[16:]
    out[...] = total


def direct(tables, pairs, swap, weight, ins, coef, entry, entries):
    size = tables[0].shape[0] // (2 if pairs == 3 else 1)
    smem = pl.BlockSpec(memory_space=pltpu.SMEM)
    vmem = pl.BlockSpec(memory_space=pltpu.VMEM)
    return pl.pallas_call(
        direct_kernel,
        in_specs=[smem, smem] + [vmem] * (3 + len(tables)),
        out_specs=vmem,
        out_shape=jax.ShapeDtypeStruct((8, entries), jnp.float32),
        scratch_shapes=[pltpu.VMEM((pairs * size, size // 2), jnp.float32)],
        cost_estimate=pl.CostEstimate(
            flops=2 * pairs * size * size * ins.shape[1] * 3,
            bytes_accessed=40 * ins.shape[1],
            transcendentals=0,
        ),
        name="direct",
    )(swap, weight, ins, coef, entry, *tables)


def after(value, *others):
    return lax.optimization_barrier((value,) + others)[0]


def total_over(value, axis):
    devices = lax.axis_size(axis)
    if devices & (devices - 1):
        return lax.psum(value, axis)
    distance = 1
    while distance < devices:
        value = value + lax.ppermute(value, axis, [(i, i ^ distance) for i in range(devices)])
        distance *= 2
    return value


def local(
    meson_fields, perambulators, direct_ins, direct_coef, direct_entry, box_ins, box_coef, box_entry
):
    devices = lax.axis_size("tm")
    owned = 4
    entries = owned * devices
    here = lax.axis_index("tm")
    role = here % GROUP
    everyone = range(devices)

    def move(value, target):
        route = [(i, target[i % GROUP](i) % devices) for i in everyone if i % GROUP in target]
        return lax.ppermute(value, "tm", route)

    def by_role(*choices):
        picked = jnp.asarray(choices[3])
        for number in range(3):
            picked = jnp.where(role == number, choices[number], picked)
        return picked

    fields = meson_fields[:, :, 0]
    factor = perambulators[:, 0]
    own = dress(fields, factor, 0, PARTS[:1])
    own = own + dress(fields, after(factor, own[0]), PARTS[0], PARTS[1:])
    count = len(own)
    half = count // 2

    across = {0: lambda i: i + 1, 1: lambda i: i + 2, 2: lambda i: i - 2, 3: lambda i: i - 1}
    along = {0: lambda i: i - GROUP, 3: lambda i: i + GROUP}
    beside = {0: lambda i: i + 1, 3: lambda i: i - 1}
    cross = {0: lambda i: i + 2, 3: lambda i: i - 2}

    terms = box_ins.shape[0]
    ins_table = box_ins.T
    swapped_table = ins_table[jnp.array([1, 0, 3, 2])]
    part = terms // 2
    late_table = jnp.where(role == 1, ins_table[:, part:], swapped_table[:, :part])
    send_table = jnp.where(role == 0, swapped_table[:, :part], ins_table[:, part:])
    late_entry = jnp.where(role == 1, box_entry[part:], box_entry[:part])
    late_coef = jnp.where(role == 1, box_coef[part:], box_coef[:part])

    near, far = [], []
    for chunk in range(count):
        near.append(move(own[chunk], across))
        far.append(move(own[chunk], along))
    rows = own[0].shape[2]
    cuts = [(j, 0, rows) for j in range(half - 1)]
    cuts += [(half - 1, 0, rows // 2), (half - 1, rows // 2, rows // 2)]
    split = [
        jnp.where(
            role == 0,
            own[half + j][:, :, start : start + length],
            own[j][:, :, start : start + length],
        )
        for j, start, length in cuts
    ]
    upper = jnp.where(role == 0, 0, 1).astype(jnp.int32)[None]
    shares = [slice(0, part // 2), slice(part // 2, part)]
    chosen = [send_table[row, share] for share in shares for row in (0, 2)]
    extra = pick(own, jnp.concatenate(chosen), upper, len(shares))
    mate = move(after(own[-1], extra[0]), beside)

    edge = (role == 0) | (role == 3)
    one, zero = jnp.float32(1.0), jnp.float32(0.0)

    def weights(first, second, third):
        return jnp.stack([first + zero, second + zero, third + zero])

    def box_table(table, entry, coef, weight, swap):
        scale = [weight[apart] * coef for apart in range(3)]
        scale.append(jnp.where(swap == 1, -one, one) * jnp.ones_like(coef))
        return jnp.concatenate([table, entry[None]]), jnp.stack(scale)

    def role_table(swap):
        return jnp.where(swap == 1, swapped_table, ins_table)

    def join(first, second):
        return tuple(jnp.concatenate([a, b], axis=1) for a, b in zip(first, second))

    outer = jnp.where(edge, one, zero)
    inner = one - outer
    same_weight = weights(one, zero, zero)
    near_weight = weights(zero, inner, outer)
    third_weight = weights(zero, by_role(zero, zero, one, zero), outer)
    split_weight = weights(zero, by_role(zero, one, zero, zero), zero)
    both_inner = weights(zero, inner, zero)
    near_swap = by_role(0, 1, 0, 1)
    third_swap = by_role(0, 0, 1, 1)
    size = 2 * fields.shape[1]
    with_entry = functools.partial(box_table, entry=box_entry, coef=box_coef)
    same_table = with_entry(ins_table, weight=same_weight, swap=0)
    near_table = with_entry(role_table(near_swap), weight=near_weight, swap=near_swap)
    third_table = with_entry(role_table(third_swap), weight=third_weight, swap=third_swap)
    both_table = join(near_table, third_table)
    late_swap = by_role(0, 0, 1, 0)
    late_ins, late_scale = box_table(late_table, late_entry, late_coef, both_inner, late_swap)
    turn = by_role(0, 0, fields.shape[2] // 2, 0) + jnp.zeros_like(late_entry)
    late_ins = jnp.concatenate([late_ins, turn[None]])
    late_tables = [(late_ins[:, share], late_scale[:, share]) for share in shares]
    main_scalars = (
        jnp.stack([jnp.int32(0), near_swap, third_swap, edge.astype(jnp.int32)]),
        jnp.concatenate([same_weight, near_weight, third_weight]),
    )
    split_scalars = (main_scalars[0], split_weight)
    direct_terms = (direct_ins.T, direct_coef[None], direct_entry[None])
    small = (
        near_table, third_table, both_table, late_tables, main_scalars, split_scalars, direct_terms
    )

    total = box([(own, own, [])], same_table, entries)
    table = jnp.zeros((2 * size, 3 * size), jnp.float32)
    (total, small, extra, split), _ = lax.optimization_barrier(((total, small, extra, split), near[0]))
    near_table, third_table, both_table, late_tables, main_scalars, split_scalars, direct_terms = small
    split_in, extra_in = [], []
    for piece in split:
        split_in.append(move(after(piece, near[-2]), cross))
    for piece in extra:
        extra_in.append(move(after(piece, near[-2]), cross))
    early = (total,)
    near_beside, far_beside = [], []
    for chunk in range(count):
        if chunk < count - 1:
            far_beside.append(move(after(far[chunk], *early), beside))
        near_beside.append(move(after(near[chunk], *early), beside))
        table = lax.cond(
            edge,
            lambda o, a, z, c, t: gram([o, a, z], 2, 3, t),
            lambda o, a, z, c, t: gram([o, a, c], 2, 3, t),
            own[chunk], near[chunk], far[chunk], near_beside[chunk], table,
        )
        early = (table,)
        if chunk == count - 2:
            total += lax.cond(
                edge,
                lambda o, m, k: jnp.zeros((8, entries), jnp.float32),
                lambda o, m, k: box([(o, m, [])], k, entries),
                own, near[:-1] + [mate], after(near_table, table),
            )
            early = (table, total)
    far_beside.append(move(after(far[-1], table), beside))
    third_table, both_table = after((third_table, both_table), table)
    third = lax.cond(
        edge,
        lambda o, a, z, c, k, j: box([(o, a, []), (a, z, [])], j, entries),
        lambda o, a, z, c, k, j: box([(o, c, [])], k, entries),
        own, near, far, near_beside, third_table, both_table,
    )
    main = direct([table], 3, *after(main_scalars, third), *direct_terms, entries)
    branch = by_role(0, 1, 2, 0)
    split_gram = after(jnp.zeros((size, size), jnp.float32), main)
    for piece, (j, start, _) in zip(split_in, cuts):
        split_gram = lax.switch(
            branch,
            [
                lambda v, lo, hi, t: jnp.zeros_like(t),
                lambda v, lo, hi, t, start=start: gram([v, lo], 1, 1, t, start),
                lambda v, lo, hi, t, start=start: gram([v, hi], 1, 1, t, start),
            ],
            piece, far_beside[j], far_beside[half + j], split_gram,
        )
    split_other = move(split_gram, {2: lambda i: i - 5})
    total += third + main
    token = split_gram
    late = []
    for number in range(len(shares)):
        token = lax.cond(
            edge,
            lambda v, f, x, k: jnp.zeros((8, entries), jnp.float32),
            lambda v, f, x, k: box([(v, f, [x])], k, entries, turned=True),
            split_in, far_beside, extra_in[number], after(late_tables[number], token),
        )
        late.append(token)
        if number == 0:
            scalars = after(split_scalars, token)
            token = lax.cond(
                role == 1,
                lambda a, b, k, d: direct([a, b], 1, *k, *d, entries),
                lambda a, b, k, d: jnp.zeros((8, entries), jnp.float32),
                split_gram, split_other, scalars, direct_terms,
            )
            late.append(token)
    total += sum(late)
    summed = total_over(total, "tm") / devices
    mine = lax.dynamic_slice_in_dim(summed[:6], here * owned, owned, axis=1)
    return mine.reshape(3, 2, owned)


def solution(mesh):
    placed = (
        P(None, None, ("cfg", "tm"), None, None),
        P(None, ("cfg", "tm"), None, None),
        P(),
        P(),
        P(),
        P(),
        P(),
        P(),
    )

    return jax.shard_map(
        local, mesh=mesh, in_specs=placed, out_specs=P(None, None, ("cfg", "tm")), check_vma=False
    )
```
